256 devices in a mesh: dp: 32 (over y, x, core), mp: 8 (over z).
Axes of the slice: x: 4, y: 4, z: 8, core: 2. Of those that a mesh axis runs over, the one named last changes fastest.
Arguments:
- hidden: bfloat16 [16384, 4096], P('dp', 'mp'), may hold values from -50 to 50
- norm_gain: float32 [4096], replicated, may hold values from 0.1 to 1.9
- w_query: bfloat16 [4096, 4096], P(None, 'mp'), may hold values from -0.09375 to 0.09375
- w_out: bfloat16 [4096, 4096], P('mp'), may hold values from -0.09375 to 0.09375
- nb_keys: bfloat16 [256, 128, 4096], P('dp', None, 'mp'), may hold values from -250 to 250
- nb_values: bfloat16 [256, 128, 4096], P('dp', None, 'mp'), may hold values from -10 to 10
- neighbours: int32 [256, 2], P('dp'), may hold values from 0 to 255, as said below
- valid_spans: int32 [32], P('dp'), may hold values from 6 to 8, as said below
Outputs:
- mixed: float32 [16384, 4096], P('dp', 'mp')
The draws below stay inside these ranges and needn't reach their ends.
Inputs may be any that keep to these rules, and one draw needn't show every extreme that they name: Block ids; block b is stored by index b // 8 of dp, its owner. The two neighbours of a span have different owners. The spans of one index of dp name one owner at most 2 times, and some owner is named exactly 2 times by the live spans of every index of dp. `valid_spans`: some index of dp has all 8 spans live.
All inputs are finite; a program needn't handle non-finite values.
Results may differ from the reference program's by a relative error of at most 0.0066.
Values may be sent and summed in bfloat16 or wider, within the bound.
No kernel may reach another device: no remote copies, remote signals or barrier semaphores. Data moves between devices by JAX's collectives and lax.ppermute only.
A program may use at most 128 MiB of HBM per device.

```python
import math
import jax
import jax.numpy as jnp
from jax import lax

D = 4096
HEADS = 32
HS = 128
SPAN = 64
NBR = 128
NB_DEV = 8
HQ = 4096
SPAN_DEV = 8
MOST = 2
TOKENS = 16384
SPANS = 256
NBLOCKS = 256


def draw_hidden(key, part):
    key_base, key_rows, key_cols = jax.random.split(key, 3)
    row_scale = jnp.exp(jax.random.uniform(key_rows, (TOKENS, 1), jnp.float32, 0.0, math.log(10.0)))
    col_scale = jnp.exp(jax.random.uniform(key_cols, (1, D), jnp.float32, 0.0, math.log(10.0)))
    base_draw = jax.random.normal(key_base, (TOKENS, D), jnp.float32)
    return (jnp.clip(base_draw, -5.0, 5.0) * row_scale * col_scale * 0.1).astype(jnp.bfloat16)


def draw_nb_keys(key, part):
    key_base = jax.random.fold_in(key, 0)
    array_shape = (NBLOCKS, NBR, HEADS * HS)
    base_draw = jnp.clip(jax.random.normal(key_base, array_shape, jnp.float32), -5.0, 5.0)
    return base_draw.astype(jnp.bfloat16)


def one_order(sub_key):
    return jax.random.permutation(sub_key, NBLOCKS // NB_DEV - 1)


def draw_neighbours(key, part):
    key_special, key_perm, key_groups, key_slots = jax.random.split(key, 4)
    owner_count = NBLOCKS // NB_DEV
    per_device = SPAN_DEV
    special = jax.random.randint(key_special, (), 0, owner_count)
    shuffled = jax.vmap(one_order)(jax.random.split(key_perm, owner_count)).astype(jnp.int32)
    owner_queue = jnp.concatenate([jnp.full((owner_count, 1), special, jnp.int32), (special + 1 + shuffled) % owner_count], axis=1)
    lowest = max(1, -((owner_count - 2 * per_device) // (MOST - 1)))
    highest = min(owner_count, 2 * per_device // MOST)
    group_count = jax.random.randint(key_groups, (owner_count, 1), lowest, highest + 1)
    position = jnp.arange(2 * per_device, dtype=jnp.int32)[None, :]
    picked = jnp.where(position < MOST * group_count, position // MOST, group_count + position - MOST * group_count)
    owners = jnp.take_along_axis(owner_queue, picked, axis=1)
    chosen = jnp.stack([owners[:, :per_device], owners[:, per_device:]], axis=-1)
    slot_ids = jax.random.randint(key_slots, (owner_count, per_device, 2), 0, NB_DEV)
    return (chosen * NB_DEV + slot_ids).reshape(SPANS, 2).astype(jnp.int32)


def draw_valid_spans(key, part):
    key_counts, key_full, key_low = jax.random.split(key, 3)
    owner_count = NBLOCKS // NB_DEV
    lowest = 3 * SPAN_DEV // 4
    counts = jax.random.randint(key_counts, (owner_count,), lowest, SPAN_DEV + 1)
    full_device = jax.random.randint(key_full, (), 0, owner_count)
    low_device = (full_device + 1 + jax.random.randint(key_low, (), 0, owner_count - 1)) % owner_count
    device_index = jnp.arange(owner_count, dtype=jnp.int32)
    counts = jnp.where(device_index == full_device, SPAN_DEV, jnp.where(device_index == low_device, lowest, counts))
    return counts.astype(jnp.int32)


def shard_levels(rng, dims, cuts, smallest, top_value):
    def one(dim, parts):
        heights = jax.random.uniform(jax.random.fold_in(jax.random.fold_in(rng, 6), dim), (parts,), jnp.float32, smallest / len(cuts), top_value / len(cuts))
        return jnp.repeat(jnp.exp(heights), dims[dim] // parts).reshape((-1,) + (1,) * (len(dims) - dim - 1))

    gain = one(*cuts[0])
    for cut in cuts[1:]:
        gain = gain * one(*cut)
    return gain


def scatter_about(own_key, dims, scale, most, shards=(), kind=jnp.bfloat16):
    values = jax.random.normal(own_key, dims, jnp.float32) * scale
    if len(shards) > 0:
        values = shard_levels(own_key, dims, shards, -0.22, 0.18) * values
    return jnp.clip(values, min=-most, max=most).astype(kind)


def setup_inputs(seed: int = 0) -> dict:
    arg_keys = jax.random.split(jax.random.key(seed), 9)
    hidden = draw_hidden(jax.random.fold_in(arg_keys[8], 71), 0)
    norm_gain = jnp.clip(1.0 + 0.18 * jax.random.normal(arg_keys[1], (D,), jnp.float32), 0.1, 1.9)
    w_query = scatter_about(arg_keys[2], (D, HQ), D ** -0.5, 0.09375, ((1, 8),))
    w_out = scatter_about(arg_keys[3], (HQ, D), HQ ** -0.5, 0.09375, ((0, 8),))
    nb_keys = draw_nb_keys(jax.random.fold_in(arg_keys[8], 71), 0)
    nb_values = scatter_about(arg_keys[5], (NBLOCKS, NBR, HQ), 2.0, 10.0, ((0, 32), (2, 8)))
    neighbours = draw_neighbours(jax.random.fold_in(arg_keys[8], 71), 0)
    valid_spans = draw_valid_spans(jax.random.fold_in(arg_keys[8], 71), 0)
    return dict(hidden=hidden, norm_gain=norm_gain, w_query=w_query, w_out=w_out, nb_keys=nb_keys, nb_values=nb_values, neighbours=neighbours, valid_spans=valid_spans)


eps = 1e-05

def attend(query_rows, key_rows, value_rows):
    query_heads = query_rows.reshape(SPAN, HEADS, HS).astype(jnp.float32)
    key_heads = key_rows.reshape(2, NBR, HEADS, HS).astype(jnp.float32)
    value_heads = value_rows.reshape(2, NBR, HEADS, HS).astype(jnp.float32)
    factor = 1.0 / math.sqrt(HS)
    scores = jnp.einsum('qhd,nkhd->nqhk', query_heads, key_heads, precision=lax.Precision.HIGHEST) * factor
    score_top = lax.optimization_barrier(jnp.max(scores, axis=-1))
    weights = jnp.exp(scores - score_top[..., None])
    weight_sum = lax.optimization_barrier(jnp.sum(weights, axis=-1))
    rounded = lax.optimization_barrier(weights.astype(jnp.bfloat16)).astype(jnp.float32)
    summed = jnp.einsum('nqhk,nkhd->nqhd', rounded, value_heads, precision=lax.Precision.HIGHEST)
    part_out = lax.optimization_barrier((summed / weight_sum[..., None]).astype(jnp.bfloat16)).astype(jnp.float32)
    best_score = lax.optimization_barrier(jnp.max(score_top, axis=0))
    mix_weight = jnp.exp(score_top - best_score[None]) * weight_sum
    merged = lax.optimization_barrier(jnp.sum(part_out * mix_weight[..., None], axis=0)) / lax.optimization_barrier(jnp.sum(mix_weight, axis=0))[..., None]
    return merged.reshape(SPAN, HEADS * HS).astype(jnp.bfloat16)

def reference(hidden, norm_gain, w_query, w_out, nb_keys, nb_values, neighbours, valid_spans):
    widened = hidden.astype(jnp.float32)
    normed = (widened * lax.rsqrt(lax.optimization_barrier(jnp.mean(widened * widened, axis=1, keepdims=True)) + eps) * norm_gain).astype(jnp.bfloat16)
    queries = jnp.dot(normed, w_query, preferred_element_type=jnp.float32).astype(jnp.bfloat16)
    inner_width = HEADS * HS
    shifted = jnp.concatenate([queries[SPAN - 1:], jnp.zeros((SPAN - 1, inner_width), jnp.bfloat16)], axis=0)
    grouped = shifted.reshape(SPANS, SPAN, inner_width)

    def one_span(span_item):
        query_rows, block_ids = span_item
        return attend(query_rows, nb_keys[block_ids], nb_values[block_ids])
    attended = lax.map(one_span, (grouped, neighbours))
    span_order = jnp.arange(SPANS, dtype=jnp.int32)
    is_live = span_order % SPAN_DEV < valid_spans[span_order // SPAN_DEV]
    attended = jnp.where(is_live[:, None, None], attended, jnp.zeros_like(attended))
    flat_rows = attended.reshape(TOKENS, inner_width)
    placed = jnp.concatenate([jnp.zeros((SPAN - 1, inner_width), jnp.bfloat16), flat_rows[:TOKENS - SPAN + 1]], axis=0)
    return widened + jnp.dot(placed, w_out, preferred_element_type=jnp.float32)
```

```python
import math

import jax
import jax.numpy as jnp
from jax import lax
from jax.experimental import pallas as pl
from jax.experimental.pallas import tpu as pltpu
from jax.sharding import PartitionSpec as P

HS = 128
SPAN = 64
SLOTS = 2
STATS = 8

eps = 1e-05
f32 = jnp.float32
bf16 = jnp.bfloat16


def shifted(block, axis, distance):
    devices = range(lax.axis_size(axis))
    route = [(i - distance, i) for i in devices if i - distance in devices]
    return lax.ppermute(block, axis, route)


def attend_kernel(ids_ref, q_ref, k_ref, v_ref, out_ref):
    peers = q_ref.shape[0]
    heads = q_ref.shape[2] // HS
    step = pl.program_id(0)
    factor = 1.0 / math.sqrt(HS)
    lane = lax.broadcasted_iota(jnp.int32, (SPAN, 128), 1)
    row = lax.broadcasted_iota(jnp.int32, (STATS, 128), 0)
    for p in range(peers):
        stats = []
        for j in range(SLOTS):
            block = ids_ref[(step * peers + p) * SLOTS + j]
            rows = pl.ds(j * SPAN, SPAN)
            stat = jnp.zeros((SPAN, 128), f32)
            for h in range(heads):
                cols = pl.ds(h * HS, HS)
                scores = lax.dot_general(
                    q_ref[p, rows, cols], k_ref[block, :, cols],
                    (((1,), (1,)), ((), ())), preferred_element_type=f32,
                ) * factor
                top = jnp.max(scores, axis=-1, keepdims=True)
                weights = jnp.exp(scores - top)
                total = jnp.sum(weights, axis=-1, keepdims=True)
                summed = jnp.dot(
                    weights.astype(bf16), v_ref[block, :, cols], preferred_element_type=f32
                )
                out_ref[p, rows, cols] = (summed / total).astype(bf16)
                stat = jnp.where(lane == h, top + jnp.log(total), stat)
            stats.append(stat)
        turned = jnp.transpose(jnp.concatenate(stats, axis=0))[:STATS]
        high = turned.astype(bf16).astype(f32)
        middle = (turned - high).astype(bf16).astype(f32)
        low = (turned - high - middle).astype(bf16).astype(f32)
        for h in range(heads):
            piece = jnp.where(
                row == 0, high[h:h + 1],
                jnp.where(row == 1, middle[h:h + 1], jnp.where(row == 2, low[h:h + 1], 0.0)),
            )
            out_ref[p, pl.ds(SLOTS * SPAN, STATS), pl.ds(h * HS, HS)] = piece.astype(bf16)


def attend(ids, asked, keys, values):
    peer_count, rows, width = asked.shape
    step = 4
    stored, tokens, _ = keys.shape
    return pl.pallas_call(
        attend_kernel,
        out_shape=jax.ShapeDtypeStruct((peer_count, rows + STATS, width), bf16),
        grid_spec=pltpu.PrefetchScalarGridSpec(
            num_scalar_prefetch=1,
            grid=(peer_count // step,),
            in_specs=[
                pl.BlockSpec((step, rows, width), lambda i, ids: (i, 0, 0)),
                pl.BlockSpec((stored, tokens, width), lambda i, ids: (0, 0, 0)),
                pl.BlockSpec((stored, tokens, width), lambda i, ids: (0, 0, 0)),
            ],
            out_specs=pl.BlockSpec((step, rows + STATS, width), lambda i, ids: (i, 0, 0)),
        ),
        compiler_params=pltpu.CompilerParams(dimension_semantics=("arbitrary",)),
        name="attend",
    )(ids, asked, keys, values)


def combine_kernel(owner_ref, rank_ref, live_ref, first_ref, second_ref, out_ref, stat_ref):
    span = pl.program_id(0)
    width = out_ref.shape[2]
    heads = width // HS
    parts = []
    for n, ref in enumerate((first_ref, second_ref)):
        offset = pl.multiple_of(rank_ref[2 * span + n] * SPAN, SPAN)
        stat = ref[0, pl.ds(SLOTS * SPAN, STATS), :].astype(f32)
        lse = stat[0:1] + stat[1:2] + stat[2:3]
        row = lax.broadcasted_iota(jnp.int32, (128, 128), 0)
        tile = jnp.zeros((128, 128), f32)
        for h in range(heads):
            tile = jnp.where(row == h, lse[:, h * HS:(h + 1) * HS], tile)
        stat_ref[n] = jnp.transpose(tile)
        parts.append((ref[0, pl.ds(offset, SPAN), :].astype(f32), stat_ref[n, pl.ds(offset, SPAN), :]))
    gap = parts[0][1] - parts[1][1]
    mine = 1.0 / (1.0 + jnp.exp(-gap))
    other = 1.0 / (1.0 + jnp.exp(gap))
    alive = span < live_ref[0]
    for h in range(heads):
        cols = slice(h * HS, (h + 1) * HS)
        merged = parts[0][0][:, cols] * mine[:, h:h + 1] + parts[1][0][:, cols] * other[:, h:h + 1]
        out_ref[0, :, cols] = jnp.where(alive, merged, 0.0).astype(bf16)


def combine(owners, ranks, live, back):
    spans = owners.shape[0] // 2
    _, rows, width = back.shape
    return pl.pallas_call(
        combine_kernel,
        out_shape=jax.ShapeDtypeStruct((spans, SPAN, width), bf16),
        grid_spec=pltpu.PrefetchScalarGridSpec(
            num_scalar_prefetch=3,
            grid=(spans,),
            in_specs=[
                pl.BlockSpec((1, rows, width), lambda i, own, rank, live: (own[2 * i], 0, 0)),
                pl.BlockSpec((1, rows, width), lambda i, own, rank, live: (own[2 * i + 1], 0, 0)),
            ],
            out_specs=pl.BlockSpec((1, SPAN, width), lambda i, own, rank, live: (i, 0, 0)),
            scratch_shapes=[pltpu.VMEM((2, 128, 128), f32)],
        ),
        compiler_params=pltpu.CompilerParams(dimension_semantics=("arbitrary",)),
        name="combine",
    )(owners, ranks, live, back, back)


def shards(hidden, norm_gain, w_query, w_out, nb_keys, nb_values, neighbours, valid_spans):
    tok_rows = hidden.shape[0]
    span_dev = tok_rows // SPAN
    stored = nb_keys.shape[0]
    inner_width = w_query.shape[1]
    peer_count = lax.axis_size("dp")
    widened = lax.all_gather(hidden, "mp", axis=1, tiled=True).astype(f32)
    normed = (
        widened * lax.rsqrt(jnp.mean(widened * widened, axis=1, keepdims=True) + eps) * norm_gain
    ).astype(bf16)
    queries = jnp.dot(normed, w_query, preferred_element_type=f32).astype(bf16)
    following = shifted(queries[: SPAN - 1], "dp", -1)
    grouped = jnp.concatenate([queries[SPAN - 1 :], following], axis=0).reshape(
        span_dev, SPAN, inner_width
    )
    live_span = jnp.arange(span_dev, dtype=jnp.int32) < valid_spans[0]
    owners = (neighbours // stored).reshape(-1)
    slot_ids = (neighbours % stored).reshape(-1)
    is_live = jnp.repeat(live_span, 2)
    req_order = jnp.arange(owners.shape[0], dtype=jnp.int32)
    earlier = (
        (owners[:, None] == owners[None, :])
        & is_live[None, :]
        & (req_order[None, :] < req_order[:, None])
    )
    slot_rank = jnp.minimum(jnp.sum(earlier.astype(jnp.int32), axis=1), SLOTS - 1)
    target = jnp.where(is_live, owners * SLOTS + slot_rank, -1)
    slot_match = target[:, None] == jnp.arange(peer_count * SLOTS, dtype=jnp.int32)[None, :]
    request_table = jnp.sum(jnp.where(slot_match, slot_ids[:, None], 0), axis=0)
    request_table = request_table.reshape(peer_count, SLOTS)
    source_span = jnp.sum(jnp.where(slot_match, req_order[:, None] // 2, 0), axis=0)
    sent_rows = grouped[source_span].reshape(peer_count, SLOTS * SPAN, inner_width)
    wanted = lax.all_to_all(request_table, "dp", split_axis=0, concat_axis=0, tiled=True)
    asked = lax.all_to_all(sent_rows, "dp", split_axis=0, concat_axis=0, tiled=True)
    answers = attend(wanted.reshape(-1), asked, nb_keys, nb_values)
    back = lax.all_to_all(answers, "dp", split_axis=0, concat_axis=0, tiled=True)
    merged = combine(owners, slot_rank, valid_spans, back)
    flat_rows = merged.reshape(tok_rows, inner_width)
    previous = shifted(flat_rows[tok_rows - SPAN + 1 :], "dp", 1)
    placed = jnp.concatenate([previous, flat_rows[: tok_rows - SPAN + 1]], axis=0)
    head_terms = jnp.dot(placed, w_out, preferred_element_type=f32).astype(bf16)
    summed = lax.psum_scatter(head_terms, "mp", scatter_dimension=1, tiled=True)
    return hidden.astype(f32) + summed.astype(f32)


def solution(mesh):
    placed = (
        P("dp", "mp"),
        P(),
        P(None, "mp"),
        P("mp", None),
        P("dp", None, "mp"),
        P("dp", None, "mp"),
        P("dp", None),
        P("dp"),
    )
    return jax.shard_map(
        shards, mesh=mesh, in_specs=placed, out_specs=P("dp", "mp"), check_vma=False
    )
```

```python
import math

import jax
import jax.numpy as jnp
from jax import lax
from jax.experimental import pallas as pl
from jax.experimental.pallas import tpu as pltpu
from jax.sharding import PartitionSpec as P

HS = 128
SPAN = 64
SLOTS = 2
STATS = 8
PARTS = 1
LANES = 128

eps = 1e-05
f32 = jnp.float32
bf16 = jnp.bfloat16


def shifted(block, axis, distance):
    devices = range(lax.axis_size(axis))
    route = [(i - distance, i) for i in devices if i - distance in devices]
    return lax.ppermute(block, axis, route)


def attend_kernel(ids_ref, q_ref, k_ref, v_ref, out_ref):
    peers, rows, width = q_ref.shape
    count = rows // SLOTS
    together = LANES // count
    groups = width // HS // together
    step = pl.program_id(0)
    factor = 1.0 / math.sqrt(HS)
    zero = jnp.zeros((count, HS), bf16)
    row = lax.broadcasted_iota(jnp.int32, (STATS, LANES), 0)
    for p in range(peers):
        for j in range(SLOTS):
            block = ids_ref[(step * peers + p) * SLOTS + j]
            tokens = pl.ds(j * count, count)
            for g in range(groups):
                first = g * together
                cols = pl.ds(first * HS, together * HS)
                spread = []
                for h in range(together):
                    line = [zero] * together
                    line[h] = q_ref[p, tokens, pl.ds((first + h) * HS, HS)]
                    spread.append(jnp.concatenate(line, axis=1))
                scores = lax.dot_general(
                    k_ref[block, :, cols], jnp.concatenate(spread, axis=0),
                    (((1,), (1,)), ((), ())), preferred_element_type=f32,
                ) * factor
                top = jnp.max(scores, axis=0, keepdims=True)
                weights = jnp.exp(scores - top)
                total = jnp.sum(weights, axis=0, keepdims=True)
                summed = lax.dot_general(
                    weights.astype(bf16), v_ref[block, :, cols],
                    (((0,), (0,)), ((), ())), preferred_element_type=f32,
                )
                scale = jnp.transpose(jnp.broadcast_to(1.0 / total, (LANES, LANES)))
                for h in range(together):
                    own = slice(h * count, (h + 1) * count)
                    piece = summed[own, h * HS:(h + 1) * HS] * scale[own]
                    out_ref[p, tokens, pl.ds((first + h) * HS, HS)] = piece.astype(bf16)
                lse = top + jnp.log(total)
                high = lse.astype(bf16).astype(f32)
                middle = (lse - high).astype(bf16).astype(f32)
                low = (lse - high - middle).astype(bf16).astype(f32)
                stat = jnp.where(
                    row == 0, high, jnp.where(row == 1, middle, jnp.where(row == 2, low, 0.0))
                )
                place = pl.ds((g * SLOTS + j) * LANES, LANES)
                out_ref[p, pl.ds(rows, STATS), place] = stat.astype(bf16)
        used = groups * SLOTS * LANES
        if used < width:
            rest = jnp.zeros((STATS, width - used), bf16)
            out_ref[p, pl.ds(rows, STATS), pl.ds(used, width - used)] = rest


def attend(ids, asked, keys, values):
    peer_count, rows, width = asked.shape
    step = 8
    stored, tokens, _ = keys.shape
    slots = peer_count * SLOTS
    return pl.pallas_call(
        attend_kernel,
        out_shape=jax.ShapeDtypeStruct((peer_count, rows + STATS, width), bf16),
        grid_spec=pltpu.PrefetchScalarGridSpec(
            num_scalar_prefetch=1,
            grid=(peer_count // step,),
            in_specs=[
                pl.BlockSpec((step, rows, width), lambda i, ids: (i, 0, 0)),
                pl.BlockSpec((stored, tokens, width), lambda i, ids: (0, 0, 0)),
                pl.BlockSpec((stored, tokens, width), lambda i, ids: (0, 0, 0)),
            ],
            out_specs=pl.BlockSpec((step, rows + STATS, width), lambda i, ids: (i, 0, 0)),
        ),
        compiler_params=pltpu.CompilerParams(dimension_semantics=("arbitrary",)),
        cost_estimate=pl.CostEstimate(
            flops=slots * 4 * LANES * LANES * width,
            bytes_accessed=4 * peer_count * rows * width,
            transcendentals=slots * LANES * LANES,
        ),
        name="attend",
    )(ids, asked, keys, values)


def combine_kernel(owner_ref, rank_ref, live_ref, back_ref, out_ref, part_ref, stat_ref, sems):
    spans, count, width = out_ref.shape
    together = LANES // count
    groups = width // HS // together
    rows = SLOTS * count
    copies = []
    for i in range(2 * spans):
        offset = pl.multiple_of(rank_ref[i] * count, count)
        source = back_ref.at[owner_ref[i]]
        copies.append((
            pltpu.make_async_copy(source.at[pl.ds(offset, count)], part_ref.at[i], sems.at[i, 0]),
            pltpu.make_async_copy(source.at[pl.ds(rows, STATS)], stat_ref.at[i], sems.at[i, 1]),
        ))
    for pair in copies:
        for copy in pair:
            copy.start()
    for s in range(spans):
        for n in range(2):
            for copy in copies[2 * s + n]:
                copy.wait()
        alive = s < live_ref[0]
        for g in range(groups):
            lses = []
            for n in range(2):
                start = pl.multiple_of((g * SLOTS + rank_ref[2 * s + n]) * LANES, LANES)
                stat = stat_ref[2 * s + n, :, pl.ds(start, LANES)].astype(f32)
                lses.append(stat[0:1] + stat[1:2] + stat[2:3])
            gap = lses[0] - lses[1]
            mine = jnp.transpose(jnp.broadcast_to(1.0 / (1.0 + jnp.exp(-gap)), (LANES, LANES)))
            other = jnp.transpose(jnp.broadcast_to(1.0 / (1.0 + jnp.exp(gap)), (LANES, LANES)))
            for h in range(together):
                own = slice(h * count, (h + 1) * count)
                cols = pl.ds((g * together + h) * HS, HS)
                merged = (
                    part_ref[2 * s, :, cols].astype(f32) * mine[own]
                    + part_ref[2 * s + 1, :, cols].astype(f32) * other[own]
                )
                out_ref[s, :, cols] = jnp.where(alive, merged, 0.0).astype(bf16)


def combine(owners, ranks, live, back):
    spans = owners.shape[0] // 2
    _, rows, width = back.shape
    count = (rows - STATS) // SLOTS
    smem = pl.BlockSpec(memory_space=pltpu.SMEM)
    return pl.pallas_call(
        combine_kernel,
        out_shape=jax.ShapeDtypeStruct((spans, count, width), bf16),
        in_specs=[smem, smem, smem, pl.BlockSpec(memory_space=pl.ANY)],
        out_specs=pl.BlockSpec(memory_space=pltpu.VMEM),
        scratch_shapes=[
            pltpu.VMEM((2 * spans, count, width), bf16),
            pltpu.VMEM((2 * spans, STATS, width), bf16),
            pltpu.SemaphoreType.DMA((2 * spans, 2)),
        ],
        cost_estimate=pl.CostEstimate(
            flops=8 * spans * count * width,
            bytes_accessed=6 * spans * count * width,
            transcendentals=0,
        ),
        name="combine",
    )(owners, ranks, live, back)


def shards(hidden, norm_gain, w_query, w_out, nb_keys, nb_values, neighbours, valid_spans):
    tok_rows, width = hidden.shape
    span_dev = tok_rows // SPAN
    stored = nb_keys.shape[0]
    inner_width = w_query.shape[1]
    peer_count = lax.axis_size("dp")
    count = SPAN // PARTS
    pieces = [
        hidden.reshape(span_dev, SPAN, width)[:, i * count:(i + 1) * count].reshape(-1, width)
        for i in range(PARTS)
    ]

    live_span = jnp.arange(span_dev, dtype=jnp.int32) < valid_spans[0]
    owners = (neighbours // stored).reshape(-1)
    slot_ids = (neighbours % stored).reshape(-1)
    is_live = jnp.repeat(live_span, 2)
    req_order = jnp.arange(owners.shape[0], dtype=jnp.int32)
    earlier = (
        (owners[:, None] == owners[None, :])
        & is_live[None, :]
        & (req_order[None, :] < req_order[:, None])
    )
    slot_rank = jnp.minimum(jnp.sum(earlier.astype(jnp.int32), axis=1), SLOTS - 1)
    target = jnp.where(is_live, owners * SLOTS + slot_rank, -1)
    slot_match = target[:, None] == jnp.arange(peer_count * SLOTS, dtype=jnp.int32)[None, :]
    request_table = jnp.sum(jnp.where(slot_match, slot_ids[:, None], 0), axis=0)
    request_table = request_table.reshape(peer_count, SLOTS)
    source_span = jnp.sum(jnp.where(slot_match, req_order[:, None] // 2, 0), axis=0)
    wanted = lax.all_to_all(request_table, "dp", split_axis=0, concat_axis=0, tiled=True)
    wanted = wanted.reshape(-1)

    def is_last(i):
        position = i * count + lax.broadcasted_iota(jnp.int32, (1, count, 1), 1)
        return position == SPAN - 1

    def ask(i):
        widened = lax.all_gather(pieces[i], "mp", axis=1, tiled=True).astype(f32)
        normed = (
            widened * lax.rsqrt(jnp.mean(widened * widened, axis=1, keepdims=True) + eps) * norm_gain
        ).astype(bf16)
        queries = jnp.dot(normed, w_query, preferred_element_type=f32).astype(bf16)
        blocks = queries.reshape(span_dev, count, inner_width)
        following = shifted(blocks[:1], "dp", -1)
        grouped = jnp.concatenate([blocks[1:], following], axis=0)
        if (i + 1) * count == SPAN:
            grouped = jnp.where(is_last(i), blocks, grouped)
        sent_rows = grouped[source_span].reshape(peer_count, SLOTS * count, inner_width)
        return lax.all_to_all(sent_rows, "dp", split_axis=0, concat_axis=0, tiled=True)

    def answer(asked):
        answers = attend(wanted, asked, nb_keys, nb_values)
        return lax.all_to_all(answers, "dp", split_axis=0, concat_axis=0, tiled=True)

    def finish(i, back):
        merged = combine(owners, slot_rank, valid_spans, back)
        previous = shifted(merged[span_dev - 1 :], "dp", 1)
        placed = jnp.concatenate([previous, merged[: span_dev - 1]], axis=0)
        if (i + 1) * count == SPAN:
            placed = jnp.where(is_last(i), merged, placed)
        placed = placed.reshape(-1, inner_width)
        head_terms = jnp.dot(placed, w_out, preferred_element_type=f32).astype(bf16)
        summed = lax.psum_scatter(head_terms, "mp", scatter_dimension=1, tiled=True)
        return summed.astype(f32).reshape(span_dev, count, width)

    asked = [ask(i) for i in range(PARTS)]
    back = [answer(one) for one in asked]
    summed = [finish(i, one) for i, one in enumerate(back)]
    summed = jnp.concatenate(summed, axis=1).reshape(tok_rows, width)
    return hidden.astype(f32) + summed


def solution(mesh):
    placed = (
        P("dp", "mp"),
        P(),
        P(None, "mp"),
        P("mp", None),
        P("dp", None, "mp"),
        P("dp", None, "mp"),
        P("dp", None),
        P("dp"),
    )
    return jax.shard_map(
        shards, mesh=mesh, in_specs=placed, out_specs=P("dp", "mp"), check_vma=False
    )
```

```python
import math

import jax
import jax.numpy as jnp
from jax import lax
from jax.experimental import pallas as pl
from jax.experimental.pallas import tpu as pltpu
from jax.sharding import PartitionSpec as P

HS = 128
SPAN = 64
SLOTS = 2
STATS = 8
PARTS = 2
LANES = 128

eps = 1e-05
f32 = jnp.float32
bf16 = jnp.bfloat16


def shifted(block, axis, distance):
    devices = range(lax.axis_size(axis))
    route = [(i - distance, i) for i in devices if i - distance in devices]
    return lax.ppermute(block, axis, route)


def attend_kernel(ids_ref, q_ref, k_ref, v_ref, out_ref):
    peers, rows, width = q_ref.shape
    count = rows // SLOTS
    together = LANES // count
    groups = width // HS // together
    step = pl.program_id(0)
    factor = 1.0 / math.sqrt(HS)
    zero = jnp.zeros((count, HS), bf16)
    row = lax.broadcasted_iota(jnp.int32, (STATS, LANES), 0)
    for p in range(peers):
        for j in range(SLOTS):
            block = ids_ref[(step * peers + p) * SLOTS + j]
            tokens = pl.ds(j * count, count)
            for g in range(groups):
                first = g * together
                cols = pl.ds(first * HS, together * HS)
                spread = []
                for h in range(together):
                    line = [zero] * together
                    line[h] = q_ref[p, tokens, pl.ds((first + h) * HS, HS)]
                    spread.append(jnp.concatenate(line, axis=1))
                scores = lax.dot_general(
                    k_ref[block, :, cols], jnp.concatenate(spread, axis=0),
                    (((1,), (1,)), ((), ())), preferred_element_type=f32,
                ) * factor
                top = jnp.max(scores, axis=0, keepdims=True)
                weights = jnp.exp(scores - top)
                total = jnp.sum(weights, axis=0, keepdims=True)
                summed = lax.dot_general(
                    weights.astype(bf16), v_ref[block, :, cols],
                    (((0,), (0,)), ((), ())), preferred_element_type=f32,
                )
                scale = jnp.transpose(jnp.broadcast_to(1.0 / total, (LANES, LANES)))
                for h in range(together):
                    own = slice(h * count, (h + 1) * count)
                    piece = summed[own, h * HS:(h + 1) * HS] * scale[own]
                    out_ref[p, tokens, pl.ds((first + h) * HS, HS)] = piece.astype(bf16)
                lse = top + jnp.log(total)
                high = lse.astype(bf16).astype(f32)
                middle = (lse - high).astype(bf16).astype(f32)
                low = (lse - high - middle).astype(bf16).astype(f32)
                stat = jnp.where(
                    row == 0, high, jnp.where(row == 1, middle, jnp.where(row == 2, low, 0.0))
                )
                place = pl.ds((g * SLOTS + j) * LANES, LANES)
                out_ref[p, pl.ds(rows, STATS), place] = stat.astype(bf16)
        used = groups * SLOTS * LANES
        if used < width:
            rest = jnp.zeros((STATS, width - used), bf16)
            out_ref[p, pl.ds(rows, STATS), pl.ds(used, width - used)] = rest


def attend(ids, asked, keys, values):
    peer_count, rows, width = asked.shape
    step = 8
    stored, tokens, _ = keys.shape
    slots = peer_count * SLOTS
    return pl.pallas_call(
        attend_kernel,
        out_shape=jax.ShapeDtypeStruct((peer_count, rows + STATS, width), bf16),
        grid_spec=pltpu.PrefetchScalarGridSpec(
            num_scalar_prefetch=1,
            grid=(peer_count // step,),
            in_specs=[
                pl.BlockSpec((step, rows, width), lambda i, ids: (i, 0, 0)),
                pl.BlockSpec((stored, tokens, width), lambda i, ids: (0, 0, 0)),
                pl.BlockSpec((stored, tokens, width), lambda i, ids: (0, 0, 0)),
            ],
            out_specs=pl.BlockSpec((step, rows + STATS, width), lambda i, ids: (i, 0, 0)),
        ),
        compiler_params=pltpu.CompilerParams(dimension_semantics=("arbitrary",)),
        cost_estimate=pl.CostEstimate(
            flops=slots * 4 * LANES * LANES * width,
            bytes_accessed=4 * peer_count * rows * width,
            transcendentals=slots * LANES * LANES,
        ),
        name="attend",
    )(ids, asked, keys, values)


def combine_kernel(owner_ref, rank_ref, live_ref, back_ref, out_ref, part_ref, stat_ref, sems):
    spans, count, width = out_ref.shape
    together = LANES // count
    groups = width // HS // together
    rows = SLOTS * count
    copies = []
    for i in range(2 * spans):
        offset = pl.multiple_of(rank_ref[i] * count, count)
        source = back_ref.at[owner_ref[i]]
        copies.append((
            pltpu.make_async_copy(source.at[pl.ds(offset, count)], part_ref.at[i], sems.at[i, 0]),
            pltpu.make_async_copy(source.at[pl.ds(rows, STATS)], stat_ref.at[i], sems.at[i, 1]),
        ))
    for pair in copies:
        for copy in pair:
            copy.start()
    for s in range(spans):
        for n in range(2):
            for copy in copies[2 * s + n]:
                copy.wait()
        alive = s < live_ref[0]
        for g in range(groups):
            lses = []
            for n in range(2):
                start = pl.multiple_of((g * SLOTS + rank_ref[2 * s + n]) * LANES, LANES)
                stat = stat_ref[2 * s + n, :, pl.ds(start, LANES)].astype(f32)
                lses.append(stat[0:1] + stat[1:2] + stat[2:3])
            gap = lses[0] - lses[1]
            mine = jnp.transpose(jnp.broadcast_to(1.0 / (1.0 + jnp.exp(-gap)), (LANES, LANES)))
            other = jnp.transpose(jnp.broadcast_to(1.0 / (1.0 + jnp.exp(gap)), (LANES, LANES)))
            for h in range(together):
                own = slice(h * count, (h + 1) * count)
                cols = pl.ds((g * together + h) * HS, HS)
                merged = (
                    part_ref[2 * s, :, cols].astype(f32) * mine[own]
                    + part_ref[2 * s + 1, :, cols].astype(f32) * other[own]
                )
                out_ref[s, :, cols] = jnp.where(alive, merged, 0.0).astype(bf16)


def combine(owners, ranks, live, back):
    spans = owners.shape[0] // 2
    _, rows, width = back.shape
    count = (rows - STATS) // SLOTS
    smem = pl.BlockSpec(memory_space=pltpu.SMEM)
    return pl.pallas_call(
        combine_kernel,
        out_shape=jax.ShapeDtypeStruct((spans, count, width), bf16),
        in_specs=[smem, smem, smem, pl.BlockSpec(memory_space=pl.ANY)],
        out_specs=pl.BlockSpec(memory_space=pltpu.VMEM),
        scratch_shapes=[
            pltpu.VMEM((2 * spans, count, width), bf16),
            pltpu.VMEM((2 * spans, STATS, width), bf16),
            pltpu.SemaphoreType.DMA((2 * spans, 2)),
        ],
        cost_estimate=pl.CostEstimate(
            flops=8 * spans * count * width,
            bytes_accessed=6 * spans * count * width,
            transcendentals=0,
        ),
        name="combine",
    )(owners, ranks, live, back)


def shards(hidden, norm_gain, w_query, w_out, nb_keys, nb_values, neighbours, valid_spans):
    tok_rows, width = hidden.shape
    span_dev = tok_rows // SPAN
    stored = nb_keys.shape[0]
    inner_width = w_query.shape[1]
    peer_count = lax.axis_size("dp")
    count = SPAN // PARTS
    pieces = [
        hidden.reshape(span_dev, SPAN, width)[:, i * count:(i + 1) * count].reshape(-1, width)
        for i in range(PARTS)
    ]

    live_span = jnp.arange(span_dev, dtype=jnp.int32) < valid_spans[0]
    owners = (neighbours // stored).reshape(-1)
    slot_ids = (neighbours % stored).reshape(-1)
    is_live = jnp.repeat(live_span, 2)
    req_order = jnp.arange(owners.shape[0], dtype=jnp.int32)
    earlier = (
        (owners[:, None] == owners[None, :])
        & is_live[None, :]
        & (req_order[None, :] < req_order[:, None])
    )
    slot_rank = jnp.minimum(jnp.sum(earlier.astype(jnp.int32), axis=1), SLOTS - 1)
    target = jnp.where(is_live, owners * SLOTS + slot_rank, -1)
    slot_match = target[:, None] == jnp.arange(peer_count * SLOTS, dtype=jnp.int32)[None, :]
    request_table = jnp.sum(jnp.where(slot_match, slot_ids[:, None], 0), axis=0)
    request_table = request_table.reshape(peer_count, SLOTS)
    source_span = jnp.sum(jnp.where(slot_match, req_order[:, None] // 2, 0), axis=0)
    wanted = lax.all_to_all(request_table, "dp", split_axis=0, concat_axis=0, tiled=True)
    wanted = wanted.reshape(-1)

    def is_last(i):
        position = i * count + lax.broadcasted_iota(jnp.int32, (1, count, 1), 1)
        return position == SPAN - 1

    def ask(i):
        widened = lax.all_gather(pieces[i], "mp", axis=1, tiled=True).astype(f32)
        normed = (
            widened * lax.rsqrt(jnp.mean(widened * widened, axis=1, keepdims=True) + eps) * norm_gain
        ).astype(bf16)
        queries = jnp.dot(normed, w_query, preferred_element_type=f32).astype(bf16)
        blocks = queries.reshape(span_dev, count, inner_width)
        following = shifted(blocks[:1], "dp", -1)
        grouped = jnp.concatenate([blocks[1:], following], axis=0)
        if (i + 1) * count == SPAN:
            grouped = jnp.where(is_last(i), blocks, grouped)
        sent_rows = grouped[source_span].reshape(peer_count, SLOTS * count, inner_width)
        return lax.all_to_all(sent_rows, "dp", split_axis=0, concat_axis=0, tiled=True)

    def answer(asked):
        answers = attend(wanted, asked, nb_keys, nb_values)
        return lax.all_to_all(answers, "dp", split_axis=0, concat_axis=0, tiled=True)

    def finish(i, back):
        merged = combine(owners, slot_rank, valid_spans, back)
        previous = shifted(merged[span_dev - 1 :], "dp", 1)
        placed = jnp.concatenate([previous, merged[: span_dev - 1]], axis=0)
        if (i + 1) * count == SPAN:
            placed = jnp.where(is_last(i), merged, placed)
        placed = placed.reshape(-1, inner_width)
        head_terms = jnp.dot(placed, w_out, preferred_element_type=f32).astype(bf16)
        summed = lax.psum_scatter(head_terms, "mp", scatter_dimension=1, tiled=True)
        return summed.astype(f32).reshape(span_dev, count, width)

    asked = [ask(i) for i in range(PARTS)]
    back = [answer(one) for one in asked]
    summed = [finish(i, one) for i, one in enumerate(back)]
    summed = jnp.concatenate(summed, axis=1).reshape(tok_rows, width)
    return hidden.astype(f32) + summed


def solution(mesh):
    placed = (
        P("dp", "mp"),
        P(),
        P(None, "mp"),
        P("mp", None),
        P("dp", None, "mp"),
        P("dp", None, "mp"),
        P("dp", None),
        P("dp"),
    )
    return jax.shard_map(
        shards, mesh=mesh, in_specs=placed, out_specs=P("dp", "mp"), check_vma=False
    )
```

```python
import math

import jax
import jax.numpy as jnp
from jax import lax
from jax.experimental import pallas as pl
from jax.experimental.pallas import tpu as pltpu
from jax.sharding import PartitionSpec as P

HS = 128
SPAN = 64
SLOTS = 2
STATS = 8
PARTS = 1
LANES = 128

eps = 1e-05
f32 = jnp.float32
bf16 = jnp.bfloat16


def shifted(block, axis, distance):
    devices = range(lax.axis_size(axis))
    route = [(i - distance, i) for i in devices if i - distance in devices]
    return lax.ppermute(block, axis, route)


def turned(block, distance):
    size = lax.axis_size("mp")
    return lax.ppermute(block, "mp", [(i, (i + distance) % size) for i in range(size)])


def project(hidden, norm_gain, w_query):
    size = lax.axis_size("mp")
    me = lax.axis_index("mp")
    rows, width = hidden.shape
    half = rows // 2
    far = size // 2

    def weights(offset):
        start = (me + offset) % size * width
        gain = lax.dynamic_slice(norm_gain, (start,), (width,))
        part = lax.dynamic_slice(w_query, (start, 0), (width, w_query.shape[1]))
        return (part.astype(f32) * gain[:, None]).astype(bf16)

    def add(sums, h, block, weight):
        wide = block.astype(f32)
        squares = jnp.sum(wide * wide, axis=1, keepdims=True)
        product = jnp.dot(block, weight, preferred_element_type=f32)
        if sums[h] is None:
            sums[h] = (squares, product)
        else:
            sums[h] = (sums[h][0] + squares, sums[h][1] + product)

    sums = [None, None]
    up = [hidden[:half], hidden[half:]]
    down = list(up)
    own = weights(0)
    for h in range(2):
        add(sums, h, up[h], own)
    for step in range(1, far):
        behind, ahead = weights(-step), weights(step)
        for h in range(2):
            up[h] = turned(up[h], 1)
            down[1 - h] = turned(down[1 - h], -1)
        for h in range(2):
            add(sums, h, up[h], behind)
            add(sums, 1 - h, down[1 - h], ahead)
    opposite = weights(far)
    add(sums, 0, turned(up[0], 1), opposite)
    add(sums, 1, turned(down[1], -1), opposite)
    total = size * width
    return jnp.concatenate(
        [product * lax.rsqrt(squares / total + eps) for squares, product in sums], axis=0
    ).astype(bf16)


def output(placed, w_out):
    size = lax.axis_size("mp")
    me = lax.axis_index("mp")
    rows = placed.shape[0]
    width = w_out.shape[1] // size
    half = rows // 2
    far = size // 2
    halves = [placed[:half], placed[half:]]

    def term(h, offset):
        start = (me + offset) % size * width
        part = lax.dynamic_slice(w_out, (0, start), (w_out.shape[0], width))
        return jnp.dot(halves[h], part, preferred_element_type=f32)

    up = [turned(term(0, far).astype(bf16), 1), None]
    down = [None, turned(term(1, -far).astype(bf16), -1)]
    for offset in range(far - 1, 0, -1):
        for h in (1, 0):
            one, two = term(h, offset), term(1 - h, -offset)
            if up[h] is not None:
                one = one + up[h].astype(f32)
            if down[1 - h] is not None:
                two = two + down[1 - h].astype(f32)
            up[h] = turned(one.astype(bf16), 1)
            down[1 - h] = turned(two.astype(bf16), -1)
    return jnp.concatenate(
        [term(h, 0) + up[h].astype(f32) + down[h].astype(f32) for h in range(2)], axis=0
    )


def attend_kernel(ids_ref, q_ref, k_ref, v_ref, out_ref):
    peers, rows, width = q_ref.shape
    count = rows // SLOTS
    together = LANES // count
    groups = width // HS // together
    step = pl.program_id(0)
    factor = 1.0 / math.sqrt(HS)
    zero = jnp.zeros((count, HS), bf16)
    row = lax.broadcasted_iota(jnp.int32, (STATS, LANES), 0)
    for p in range(peers):
        for j in range(SLOTS):
            block = ids_ref[(step * peers + p) * SLOTS + j]
            tokens = pl.ds(j * count, count)
            for g in range(groups):
                first = g * together
                cols = pl.ds(first * HS, together * HS)
                spread = []
                for h in range(together):
                    line = [zero] * together
                    line[h] = q_ref[p, tokens, pl.ds((first + h) * HS, HS)]
                    spread.append(jnp.concatenate(line, axis=1))
                scores = lax.dot_general(
                    k_ref[block, :, cols], jnp.concatenate(spread, axis=0),
                    (((1,), (1,)), ((), ())), preferred_element_type=f32,
                ) * factor
                top = jnp.max(scores, axis=0, keepdims=True)
                weights = jnp.exp(scores - top)
                total = jnp.sum(weights, axis=0, keepdims=True)
                summed = lax.dot_general(
                    weights.astype(bf16), v_ref[block, :, cols],
                    (((0,), (0,)), ((), ())), preferred_element_type=f32,
                )
                scale = jnp.transpose(jnp.broadcast_to(1.0 / total, (LANES, LANES)))
                for h in range(together):
                    own = slice(h * count, (h + 1) * count)
                    piece = summed[own, h * HS:(h + 1) * HS] * scale[own]
                    out_ref[p, tokens, pl.ds((first + h) * HS, HS)] = piece.astype(bf16)
                lse = top + jnp.log(total)
                high = lse.astype(bf16).astype(f32)
                middle = (lse - high).astype(bf16).astype(f32)
                low = (lse - high - middle).astype(bf16).astype(f32)
                stat = jnp.where(
                    row == 0, high, jnp.where(row == 1, middle, jnp.where(row == 2, low, 0.0))
                )
                place = pl.ds((g * SLOTS + j) * LANES, LANES)
                out_ref[p, pl.ds(rows, STATS), place] = stat.astype(bf16)
        used = groups * SLOTS * LANES
        if used < width:
            rest = jnp.zeros((STATS, width - used), bf16)
            out_ref[p, pl.ds(rows, STATS), pl.ds(used, width - used)] = rest


def attend(ids, asked, keys, values):
    peer_count, rows, width = asked.shape
    step = 8
    stored, tokens, _ = keys.shape
    slots = peer_count * SLOTS
    return pl.pallas_call(
        attend_kernel,
        out_shape=jax.ShapeDtypeStruct((peer_count, rows + STATS, width), bf16),
        grid_spec=pltpu.PrefetchScalarGridSpec(
            num_scalar_prefetch=1,
            grid=(peer_count // step,),
            in_specs=[
                pl.BlockSpec((step, rows, width), lambda i, ids: (i, 0, 0)),
                pl.BlockSpec((stored, tokens, width), lambda i, ids: (0, 0, 0)),
                pl.BlockSpec((stored, tokens, width), lambda i, ids: (0, 0, 0)),
            ],
            out_specs=pl.BlockSpec((step, rows + STATS, width), lambda i, ids: (i, 0, 0)),
        ),
        compiler_params=pltpu.CompilerParams(dimension_semantics=("arbitrary",)),
        cost_estimate=pl.CostEstimate(
            flops=slots * 4 * LANES * LANES * width,
            bytes_accessed=4 * peer_count * rows * width,
            transcendentals=slots * LANES * LANES,
        ),
        name="attend",
    )(ids, asked, keys, values)


def combine_kernel(owner_ref, rank_ref, live_ref, back_ref, out_ref, part_ref, stat_ref, sems):
    spans, count, width = out_ref.shape
    together = LANES // count
    groups = width // HS // together
    rows = SLOTS * count
    copies = []
    for i in range(2 * spans):
        offset = pl.multiple_of(rank_ref[i] * count, count)
        source = back_ref.at[owner_ref[i]]
        copies.append((
            pltpu.make_async_copy(source.at[pl.ds(offset, count)], part_ref.at[i], sems.at[i, 0]),
            pltpu.make_async_copy(source.at[pl.ds(rows, STATS)], stat_ref.at[i], sems.at[i, 1]),
        ))
    for pair in copies:
        for copy in pair:
            copy.start()
    for s in range(spans):
        for n in range(2):
            for copy in copies[2 * s + n]:
                copy.wait()
        alive = s < live_ref[0]
        for g in range(groups):
            lses = []
            for n in range(2):
                start = pl.multiple_of((g * SLOTS + rank_ref[2 * s + n]) * LANES, LANES)
                stat = stat_ref[2 * s + n, :, pl.ds(start, LANES)].astype(f32)
                lses.append(stat[0:1] + stat[1:2] + stat[2:3])
            gap = lses[0] - lses[1]
            mine = jnp.transpose(jnp.broadcast_to(1.0 / (1.0 + jnp.exp(-gap)), (LANES, LANES)))
            other = jnp.transpose(jnp.broadcast_to(1.0 / (1.0 + jnp.exp(gap)), (LANES, LANES)))
            for h in range(together):
                own = slice(h * count, (h + 1) * count)
                cols = pl.ds((g * together + h) * HS, HS)
                merged = (
                    part_ref[2 * s, :, cols].astype(f32) * mine[own]
                    + part_ref[2 * s + 1, :, cols].astype(f32) * other[own]
                )
                out_ref[s, :, cols] = jnp.where(alive, merged, 0.0).astype(bf16)


def combine(owners, ranks, live, back):
    spans = owners.shape[0] // 2
    _, rows, width = back.shape
    count = (rows - STATS) // SLOTS
    smem = pl.BlockSpec(memory_space=pltpu.SMEM)
    return pl.pallas_call(
        combine_kernel,
        out_shape=jax.ShapeDtypeStruct((spans, count, width), bf16),
        in_specs=[smem, smem, smem, pl.BlockSpec(memory_space=pl.ANY)],
        out_specs=pl.BlockSpec(memory_space=pltpu.VMEM),
        scratch_shapes=[
            pltpu.VMEM((2 * spans, count, width), bf16),
            pltpu.VMEM((2 * spans, STATS, width), bf16),
            pltpu.SemaphoreType.DMA((2 * spans, 2)),
        ],
        cost_estimate=pl.CostEstimate(
            flops=8 * spans * count * width,
            bytes_accessed=6 * spans * count * width,
            transcendentals=0,
        ),
        name="combine",
    )(owners, ranks, live, back)


def shards(hidden, norm_gain, w_query, w_out, nb_keys, nb_values, neighbours, valid_spans):
    tok_rows, width = hidden.shape
    span_dev = tok_rows // SPAN
    stored = nb_keys.shape[0]
    inner_width = w_query.shape[1]
    peer_count = lax.axis_size("dp")
    count = SPAN // PARTS
    live_span = jnp.arange(span_dev, dtype=jnp.int32) < valid_spans[0]
    owners = (neighbours // stored).reshape(-1)
    slot_ids = (neighbours % stored).reshape(-1)
    is_live = jnp.repeat(live_span, 2)
    req_order = jnp.arange(owners.shape[0], dtype=jnp.int32)
    earlier = (
        (owners[:, None] == owners[None, :])
        & is_live[None, :]
        & (req_order[None, :] < req_order[:, None])
    )
    slot_rank = jnp.minimum(jnp.sum(earlier.astype(jnp.int32), axis=1), SLOTS - 1)
    target = jnp.where(is_live, owners * SLOTS + slot_rank, -1)
    slot_match = target[:, None] == jnp.arange(peer_count * SLOTS, dtype=jnp.int32)[None, :]
    request_table = jnp.sum(jnp.where(slot_match, slot_ids[:, None], 0), axis=0)
    request_table = request_table.reshape(peer_count, SLOTS)
    source_span = jnp.sum(jnp.where(slot_match, req_order[:, None] // 2, 0), axis=0)
    wanted = lax.all_to_all(request_table, "dp", split_axis=0, concat_axis=0, tiled=True)
    wanted = wanted.reshape(-1)

    def is_last(i):
        position = i * count + lax.broadcasted_iota(jnp.int32, (1, count, 1), 1)
        return position == SPAN - 1

    def ask(i):
        queries = project(hidden, norm_gain, w_query)
        blocks = queries.reshape(span_dev, count, inner_width)
        following = shifted(blocks[:1], "dp", -1)
        grouped = jnp.concatenate([blocks[1:], following], axis=0)
        if (i + 1) * count == SPAN:
            grouped = jnp.where(is_last(i), blocks, grouped)
        sent_rows = grouped[source_span].reshape(peer_count, SLOTS * count, inner_width)
        return lax.all_to_all(sent_rows, "dp", split_axis=0, concat_axis=0, tiled=True)

    def answer(asked):
        answers = attend(wanted, asked, nb_keys, nb_values)
        return lax.all_to_all(answers, "dp", split_axis=0, concat_axis=0, tiled=True)

    def finish(i, back):
        merged = combine(owners, slot_rank, valid_spans, back)
        previous = shifted(merged[span_dev - 1 :], "dp", 1)
        placed = jnp.concatenate([previous, merged[: span_dev - 1]], axis=0)
        if (i + 1) * count == SPAN:
            placed = jnp.where(is_last(i), merged, placed)
        placed = placed.reshape(-1, inner_width)
        return output(placed, w_out).reshape(span_dev, count, width)

    asked = [ask(i) for i in range(PARTS)]
    back = [answer(one) for one in asked]
    summed = [finish(i, one) for i, one in enumerate(back)]
    summed = jnp.concatenate(summed, axis=1).reshape(tok_rows, width)
    return hidden.astype(f32) + summed


def solution(mesh):
    placed = (
        P("dp", "mp"),
        P(),
        P(None, "mp"),
        P("mp", None),
        P("dp", None, "mp"),
        P("dp", None, "mp"),
        P("dp", None),
        P("dp"),
    )
    return jax.shard_map(
        shards, mesh=mesh, in_specs=placed, out_specs=P("dp", "mp"), check_vma=False
    )
```

```python
import math

import jax
import jax.numpy as jnp
from jax import lax
from jax.experimental import pallas as pl
from jax.experimental.pallas import tpu as pltpu
from jax.sharding import PartitionSpec as P

HS = 128
SPAN = 64
SLOTS = 2
STATS = 8
PARTS = 2
LANES = 128

eps = 1e-05
f32 = jnp.float32
bf16 = jnp.bfloat16


def shifted(block, axis, distance):
    devices = range(lax.axis_size(axis))
    route = [(i - distance, i) for i in devices if i - distance in devices]
    return lax.ppermute(block, axis, route)


def turned(block, distance):
    size = lax.axis_size("mp")
    return lax.ppermute(block, "mp", [(i, (i + distance) % size) for i in range(size)])


def project(hidden, norm_gain, w_query):
    size = lax.axis_size("mp")
    me = lax.axis_index("mp")
    rows, width = hidden.shape
    half = rows // 2
    far = size // 2

    def weights(offset):
        start = (me + offset) % size * width
        gain = lax.dynamic_slice(norm_gain, (start,), (width,))
        part = lax.dynamic_slice(w_query, (start, 0), (width, w_query.shape[1]))
        return (part.astype(f32) * gain[:, None]).astype(bf16)

    def terms(block, offset):
        wide = block.astype(f32)
        squares = jnp.sum(wide * wide, axis=1, keepdims=True)
        return squares, jnp.dot(block, weights(offset), preferred_element_type=f32)

    squares, product = terms(hidden, 0)
    up = down = hidden
    for step in range(1, far):
        up, down = turned(up, 1), turned(down, -1)
        for block, offset in ((up, -step), (down, step)):
            more = terms(block, offset)
            squares, product = squares + more[0], product + more[1]
    nearly = up
    last = jnp.concatenate([turned(up[:half], 1), turned(down[half:], -1)], axis=0)
    more = terms(last, far)
    squares, product = squares + more[0], product + more[1]
    total = size * width
    return (product * lax.rsqrt(squares / total + eps)).astype(bf16), nearly


def output(placed, w_out):
    size = lax.axis_size("mp")
    me = lax.axis_index("mp")
    rows = placed.shape[0]
    width = w_out.shape[1] // size
    half = rows // 2
    far = size // 2

    def term(block, offset):
        start = (me + offset) % size * width
        part = lax.dynamic_slice(w_out, (0, start), (w_out.shape[0], width))
        return jnp.dot(block, part, preferred_element_type=f32)

    opposite = term(placed, far).astype(bf16)
    up, down = turned(opposite[:half], 1), turned(opposite[half:], -1)
    none = jnp.zeros_like(up)
    up = jnp.concatenate([up, none], axis=0)
    down = jnp.concatenate([none, down], axis=0)
    for offset in range(far - 1, 0, -1):
        one = term(placed, offset) + up.astype(f32)
        two = term(placed, -offset) + down.astype(f32)
        up, down = turned(one.astype(bf16), 1), turned(two.astype(bf16), -1)
    return term(placed, 0) + up.astype(f32) + down.astype(f32)


def attend_kernel(ids_ref, q_ref, k_ref, v_ref, out_ref):
    peers, rows, width = q_ref.shape
    count = rows // SLOTS
    together = LANES // count
    groups = width // HS // together
    step = pl.program_id(0)
    factor = 1.0 / math.sqrt(HS)
    zero = jnp.zeros((count, HS), bf16)
    row = lax.broadcasted_iota(jnp.int32, (STATS, LANES), 0)
    for p in range(peers):
        for j in range(SLOTS):
            block = ids_ref[(step * peers + p) * SLOTS + j]
            tokens = pl.ds(j * count, count)
            for g in range(groups):
                first = g * together
                cols = pl.ds(first * HS, together * HS)
                spread = []
                for h in range(together):
                    line = [zero] * together
                    line[h] = q_ref[p, tokens, pl.ds((first + h) * HS, HS)]
                    spread.append(jnp.concatenate(line, axis=1))
                scores = lax.dot_general(
                    k_ref[block, :, cols], jnp.concatenate(spread, axis=0),
                    (((1,), (1,)), ((), ())), preferred_element_type=f32,
                ) * factor
                top = jnp.max(scores, axis=0, keepdims=True)
                weights = jnp.exp(scores - top)
                total = jnp.sum(weights, axis=0, keepdims=True)
                summed = lax.dot_general(
                    weights.astype(bf16), v_ref[block, :, cols],
                    (((0,), (0,)), ((), ())), preferred_element_type=f32,
                )
                scale = jnp.transpose(jnp.broadcast_to(1.0 / total, (LANES, LANES)))
                for h in range(together):
                    own = slice(h * count, (h + 1) * count)
                    piece = summed[own, h * HS:(h + 1) * HS] * scale[own]
                    out_ref[p, tokens, pl.ds((first + h) * HS, HS)] = piece.astype(bf16)
                lse = top + jnp.log(total)
                high = lse.astype(bf16).astype(f32)
                middle = (lse - high).astype(bf16).astype(f32)
                low = (lse - high - middle).astype(bf16).astype(f32)
                stat = jnp.where(
                    row == 0, high, jnp.where(row == 1, middle, jnp.where(row == 2, low, 0.0))
                )
                place = pl.ds((g * SLOTS + j) * LANES, LANES)
                out_ref[p, pl.ds(rows, STATS), place] = stat.astype(bf16)
        used = groups * SLOTS * LANES
        if used < width:
            rest = jnp.zeros((STATS, width - used), bf16)
            out_ref[p, pl.ds(rows, STATS), pl.ds(used, width - used)] = rest


def attend(ids, asked, keys, values):
    peer_count, rows, width = asked.shape
    step = 4
    stored, tokens, _ = keys.shape
    slots = peer_count * SLOTS
    return pl.pallas_call(
        attend_kernel,
        out_shape=jax.ShapeDtypeStruct((peer_count, rows + STATS, width), bf16),
        grid_spec=pltpu.PrefetchScalarGridSpec(
            num_scalar_prefetch=1,
            grid=(peer_count // step,),
            in_specs=[
                pl.BlockSpec((step, rows, width), lambda i, ids: (i, 0, 0)),
                pl.BlockSpec((stored, tokens, width), lambda i, ids: (0, 0, 0)),
                pl.BlockSpec((stored, tokens, width), lambda i, ids: (0, 0, 0)),
            ],
            out_specs=pl.BlockSpec((step, rows + STATS, width), lambda i, ids: (i, 0, 0)),
        ),
        compiler_params=pltpu.CompilerParams(dimension_semantics=("arbitrary",)),
        cost_estimate=pl.CostEstimate(
            flops=slots * 4 * LANES * LANES * width,
            bytes_accessed=4 * peer_count * rows * width,
            transcendentals=slots * LANES * LANES,
        ),
        name="attend",
    )(ids, asked, keys, values)


def combine_kernel(owner_ref, rank_ref, live_ref, back_ref, out_ref, part_ref, stat_ref, sems):
    spans, count, width = out_ref.shape
    together = LANES // count
    groups = width // HS // together
    rows = SLOTS * count
    copies = []
    for i in range(2 * spans):
        offset = pl.multiple_of(rank_ref[i] * count, count)
        source = back_ref.at[owner_ref[i]]
        copies.append((
            pltpu.make_async_copy(source.at[pl.ds(offset, count)], part_ref.at[i], sems.at[i, 0]),
            pltpu.make_async_copy(source.at[pl.ds(rows, STATS)], stat_ref.at[i], sems.at[i, 1]),
        ))
    for pair in copies:
        for copy in pair:
            copy.start()
    for s in range(spans):
        for n in range(2):
            for copy in copies[2 * s + n]:
                copy.wait()
        alive = s < live_ref[0]
        for g in range(groups):
            lses = []
            for n in range(2):
                start = pl.multiple_of((g * SLOTS + rank_ref[2 * s + n]) * LANES, LANES)
                stat = stat_ref[2 * s + n, :, pl.ds(start, LANES)].astype(f32)
                lses.append(stat[0:1] + stat[1:2] + stat[2:3])
            gap = lses[0] - lses[1]
            mine = jnp.transpose(jnp.broadcast_to(1.0 / (1.0 + jnp.exp(-gap)), (LANES, LANES)))
            other = jnp.transpose(jnp.broadcast_to(1.0 / (1.0 + jnp.exp(gap)), (LANES, LANES)))
            for h in range(together):
                own = slice(h * count, (h + 1) * count)
                cols = pl.ds((g * together + h) * HS, HS)
                merged = (
                    part_ref[2 * s, :, cols].astype(f32) * mine[own]
                    + part_ref[2 * s + 1, :, cols].astype(f32) * other[own]
                )
                out_ref[s, :, cols] = jnp.where(alive, merged, 0.0).astype(bf16)


def combine(owners, ranks, live, back):
    spans = owners.shape[0] // 2
    _, rows, width = back.shape
    count = (rows - STATS) // SLOTS
    smem = pl.BlockSpec(memory_space=pltpu.SMEM)
    return pl.pallas_call(
        combine_kernel,
        out_shape=jax.ShapeDtypeStruct((spans, count, width), bf16),
        in_specs=[smem, smem, smem, pl.BlockSpec(memory_space=pl.ANY)],
        out_specs=pl.BlockSpec(memory_space=pltpu.VMEM),
        scratch_shapes=[
            pltpu.VMEM((2 * spans, count, width), bf16),
            pltpu.VMEM((2 * spans, STATS, width), bf16),
            pltpu.SemaphoreType.DMA((2 * spans, 2)),
        ],
        cost_estimate=pl.CostEstimate(
            flops=8 * spans * count * width,
            bytes_accessed=6 * spans * count * width,
            transcendentals=0,
        ),
        name="combine",
    )(owners, ranks, live, back)


def shards(hidden, norm_gain, w_query, w_out, nb_keys, nb_values, neighbours, valid_spans):
    tok_rows, width = hidden.shape
    span_dev = tok_rows // SPAN
    stored = nb_keys.shape[0]
    inner_width = w_query.shape[1]
    peer_count = lax.axis_size("dp")
    count = SPAN // PARTS
    pieces = [
        hidden.reshape(span_dev, SPAN, width)[:, i * count:(i + 1) * count].reshape(-1, width)
        for i in range(PARTS)
    ]

    live_span = jnp.arange(span_dev, dtype=jnp.int32) < valid_spans[0]
    owners = (neighbours // stored).reshape(-1)
    slot_ids = (neighbours % stored).reshape(-1)
    is_live = jnp.repeat(live_span, 2)
    req_order = jnp.arange(owners.shape[0], dtype=jnp.int32)
    earlier = (
        (owners[:, None] == owners[None, :])
        & is_live[None, :]
        & (req_order[None, :] < req_order[:, None])
    )
    slot_rank = jnp.minimum(jnp.sum(earlier.astype(jnp.int32), axis=1), SLOTS - 1)
    target = jnp.where(is_live, owners * SLOTS + slot_rank, -1)
    slot_match = target[:, None] == jnp.arange(peer_count * SLOTS, dtype=jnp.int32)[None, :]
    request_table = jnp.sum(jnp.where(slot_match, slot_ids[:, None], 0), axis=0)
    request_table = request_table.reshape(peer_count, SLOTS)
    source_span = jnp.sum(jnp.where(slot_match, req_order[:, None] // 2, 0), axis=0)
    wanted = lax.all_to_all(request_table, "dp", split_axis=0, concat_axis=0, tiled=True)
    wanted = wanted.reshape(-1)

    def is_last(i):
        position = i * count + lax.broadcasted_iota(jnp.int32, (1, count, 1), 1)
        return position == SPAN - 1

    def request(i, piece):
        queries, nearly = project(piece, norm_gain, w_query)
        blocks = queries.reshape(span_dev, count, inner_width)
        following = shifted(blocks[:1], "dp", -1)
        grouped = jnp.concatenate([blocks[1:], following], axis=0)
        if (i + 1) * count == SPAN:
            grouped = jnp.where(is_last(i), blocks, grouped)
        return grouped[source_span].reshape(peer_count, SLOTS * count, inner_width), nearly

    def exchange(rows):
        return lax.all_to_all(rows, "dp", split_axis=0, concat_axis=0, tiled=True)

    def finish(i, back):
        merged = combine(owners, slot_rank, valid_spans, back)
        previous = shifted(merged[span_dev - 1 :], "dp", 1)
        placed = jnp.concatenate([previous, merged[: span_dev - 1]], axis=0)
        if (i + 1) * count == SPAN:
            placed = jnp.where(is_last(i), merged, placed)
        placed = placed.reshape(-1, inner_width)
        return output(placed, w_out).reshape(span_dev, count, width)

    sent_0, nearly = request(0, pieces[0])
    piece_1, _, wanted = lax.optimization_barrier((pieces[1], nearly, wanted))
    asked_0 = exchange(sent_0)
    sent_1, _ = request(1, piece_1)
    asked_0, sent_1 = lax.optimization_barrier((asked_0, sent_1))
    asked_1 = exchange(sent_1)
    answers_0 = attend(wanted, asked_0, nb_keys, nb_values)
    back_0 = exchange(answers_0)
    answers_1 = attend(wanted, asked_1, nb_keys, nb_values)
    back_0, answers_1 = lax.optimization_barrier((back_0, answers_1))
    back_1 = exchange(answers_1)
    summed = jnp.concatenate([finish(0, back_0), finish(1, back_1)], axis=1)
    return hidden.astype(f32) + summed.reshape(tok_rows, width)


def solution(mesh):
    placed = (
        P("dp", "mp"),
        P(),
        P(None, "mp"),
        P("mp", None),
        P("dp", None, "mp"),
        P("dp", None, "mp"),
        P("dp", None),
        P("dp"),
    )
    return jax.shard_map(
        shards, mesh=mesh, in_specs=placed, out_specs=P("dp", "mp"), check_vma=False
    )
```

```python
import functools
import math

import jax
import jax.numpy as jnp
from jax import lax
from jax.experimental import pallas as pl
from jax.experimental.pallas import tpu as pltpu
from jax.sharding import PartitionSpec as P

HS = 128
SPAN = 64
SLOTS = 2
STATS = 8
PARTS = 2
LANES = 128

eps = 1e-05
f32 = jnp.float32
bf16 = jnp.bfloat16


def shifted(block, axis, distance):
    devices = range(lax.axis_size(axis))
    route = [(i - distance, i) for i in devices if i - distance in devices]
    return lax.ppermute(block, axis, route)


def turned(block, distance):
    size = lax.axis_size("mp")
    return lax.ppermute(block, "mp", [(i, (i + distance) % size) for i in range(size)])


def near_kernel(starts_ref, gain_ref, w_ref, *refs):
    blocks, (product_ref, squares_ref) = refs[:-2], refs[-2:]
    for i, block_ref in enumerate(blocks):
        width = block_ref.shape[1]
        start = pl.multiple_of(starts_ref[i], width)
        wide = block_ref[...].astype(f32)
        scaled = (wide * gain_ref[:, pl.ds(start, width)]).astype(bf16)
        squares = wide * wide
        squares = sum(squares[:, c:c + LANES] for c in range(0, width, LANES))
        product = jnp.dot(scaled, w_ref[pl.ds(start, width), :], preferred_element_type=f32)
        if i == 0:
            product_ref[...] = product
            squares_ref[...] = squares
        else:
            product_ref[...] += product
            squares_ref[...] += squares


def far_kernel(features, place_ref, gain_ref, w_ref, up_ref, down_ref, product_ref, squares_ref, out_ref):
    half = up_ref.shape[0]
    for i, block_ref in enumerate((up_ref, down_ref)):
        rows = pl.ds(i * half, half)
        wide = block_ref[...].astype(f32)
        scaled = (wide * gain_ref[...]).astype(bf16)
        mean = jnp.sum(wide * wide, axis=1, keepdims=True)
        mean = (mean + jnp.sum(squares_ref[rows, :], axis=1, keepdims=True)) / features
        product = jnp.dot(scaled, w_ref[...], preferred_element_type=f32)
        product = (product + product_ref[rows, :]) * lax.rsqrt(mean + eps)
        out_ref[rows, :] = product.astype(bf16)


def project(hidden, norm_gain, w_query):
    size = lax.axis_size("mp")
    me = lax.axis_index("mp")
    rows, width = hidden.shape
    half = rows // 2
    far = size // 2
    smem = pl.BlockSpec(memory_space=pltpu.SMEM)
    vmem = pl.BlockSpec(memory_space=pltpu.VMEM)
    gain = norm_gain.reshape(1, -1)
    offsets = [0]
    near = [hidden]
    up = down = hidden
    for step in range(1, far):
        up, down = turned(up, 1), turned(down, -1)
        near += [up, down]
        offsets += [-step, step]
    nearly = up
    up, down = turned(up[:half], 1), turned(down[half:], -1)
    order = jnp.asarray(offsets, jnp.int32)
    product, squares = pl.pallas_call(
        near_kernel,
        out_shape=[
            jax.ShapeDtypeStruct((rows, w_query.shape[1]), f32),
            jax.ShapeDtypeStruct((rows, LANES), f32),
        ],
        in_specs=[smem] + [vmem] * (2 + len(near)),
        out_specs=[vmem, vmem],
        cost_estimate=pl.CostEstimate(
            flops=2 * rows * w_query.size, bytes_accessed=4 * w_query.size, transcendentals=0
        ),
        name="near",
    )((me + order) % size * width, gain, w_query, *near)
    inner = w_query.shape[1]
    queries = pl.pallas_call(
        functools.partial(far_kernel, size * width),
        out_shape=jax.ShapeDtypeStruct((rows, inner), bf16),
        grid_spec=pltpu.PrefetchScalarGridSpec(
            num_scalar_prefetch=1,
            grid=(1,),
            in_specs=[
                pl.BlockSpec((1, width), lambda i, place: (0, place[0])),
                pl.BlockSpec((width, inner), lambda i, place: (place[0], 0)),
                pl.BlockSpec((half, width), lambda i, place: (0, 0)),
                pl.BlockSpec((half, width), lambda i, place: (0, 0)),
                pl.BlockSpec((rows, inner), lambda i, place: (0, 0)),
                pl.BlockSpec((rows, LANES), lambda i, place: (0, 0)),
            ],
            out_specs=pl.BlockSpec((rows, inner), lambda i, place: (0, 0)),
        ),
        cost_estimate=pl.CostEstimate(
            flops=2 * rows * width * inner, bytes_accessed=4 * width * inner, transcendentals=0
        ),
        name="far",
    )((me + jnp.full((1,), far, jnp.int32)) % size, gain, w_query, up, down, product, squares)
    return queries, nearly


def output(placed, w_out):
    size = lax.axis_size("mp")
    me = lax.axis_index("mp")
    rows = placed.shape[0]
    width = w_out.shape[1] // size
    half = rows // 2
    far = size // 2

    def term(block, offset):
        start = (me + offset) % size * width
        part = lax.dynamic_slice(w_out, (0, start), (w_out.shape[0], width))
        return jnp.dot(block, part, preferred_element_type=f32)

    opposite = term(placed, far).astype(bf16)
    up, down = turned(opposite[:half], 1), turned(opposite[half:], -1)
    none = jnp.zeros_like(up)
    up = jnp.concatenate([up, none], axis=0)
    down = jnp.concatenate([none, down], axis=0)
    for offset in range(far - 1, 0, -1):
        one = term(placed, offset) + up.astype(f32)
        two = term(placed, -offset) + down.astype(f32)
        late = one.astype(bf16), two.astype(bf16)
        up, down = turned(late[0], 1), turned(late[1], -1)
    return term(placed, 0) + up.astype(f32) + down.astype(f32), late


def place_kernel(turn, source_ref, ids_ref, blocks_ref, next_ref, out_ref, group_ref):
    peers, rows, width = out_ref.shape
    spans, count, _ = blocks_ref.shape
    step = pl.program_id(0)

    @pl.when(step == 0)
    def _():
        for s in range(spans):
            rest = blocks_ref[s + 1] if s + 1 < spans else next_ref[0]
            if turn:
                position = lax.broadcasted_iota(jnp.int32, (count, width), 0)
                rest = jnp.where(position == count - 1, blocks_ref[s], rest)
            group_ref[s] = rest

    for p in range(peers):
        for j in range(SLOTS):
            slot = (step * peers + p) * SLOTS + j
            out_ref[p, pl.ds(j * count, count), :] = group_ref[source_ref[slot]]
        if rows > SLOTS * count:
            lane = lax.broadcasted_iota(jnp.int32, (STATS, width), 1)
            slot = (step * peers + p) * SLOTS
            line = jnp.where(lane == 0, ids_ref[slot], jnp.where(lane == 1, ids_ref[slot + 1], 0))
            out_ref[p, pl.ds(SLOTS * count, STATS), :] = line.astype(f32).astype(bf16)


def place(turn, with_ids, source_span, ids, blocks, following):
    spans, count, width = blocks.shape
    slots = source_span.shape[0]
    peer_count = slots // SLOTS
    step = 8
    rows = SLOTS * count + (STATS if with_ids else 0)
    return pl.pallas_call(
        functools.partial(place_kernel, turn),
        out_shape=jax.ShapeDtypeStruct((peer_count, rows, width), bf16),
        grid_spec=pltpu.PrefetchScalarGridSpec(
            num_scalar_prefetch=2,
            grid=(peer_count // step,),
            in_specs=[
                pl.BlockSpec((spans, count, width), lambda i, source, ids: (0, 0, 0)),
                pl.BlockSpec((1, count, width), lambda i, source, ids: (0, 0, 0)),
            ],
            out_specs=pl.BlockSpec((step, rows, width), lambda i, source, ids: (i, 0, 0)),
            scratch_shapes=[pltpu.VMEM((spans, count, width), bf16)],
        ),
        compiler_params=pltpu.CompilerParams(dimension_semantics=("arbitrary",)),
        cost_estimate=pl.CostEstimate(
            flops=0, bytes_accessed=2 * peer_count * rows * width, transcendentals=0
        ),
        name="place",
    )(source_span, ids, blocks, following)


def attend_kernel(ids_ref, q_ref, k_ref, v_ref, out_ref):
    peers, rows, width = out_ref.shape
    rows -= STATS
    count = rows // SLOTS
    together = LANES // count
    groups = width // HS // together
    step = pl.program_id(0)
    factor = 1.0 / math.sqrt(HS)
    zero = jnp.zeros((count, HS), bf16)
    row = lax.broadcasted_iota(jnp.int32, (STATS, LANES), 0)
    for p in range(peers):
        for j in range(SLOTS):
            block = ids_ref[(step * peers + p) * SLOTS + j]
            tokens = pl.ds(j * count, count)
            for g in range(groups):
                first = g * together
                cols = pl.ds(first * HS, together * HS)
                spread = []
                for h in range(together):
                    line = [zero] * together
                    line[h] = q_ref[p, tokens, pl.ds((first + h) * HS, HS)]
                    spread.append(jnp.concatenate(line, axis=1))
                scores = lax.dot_general(
                    k_ref[block, :, cols], jnp.concatenate(spread, axis=0),
                    (((1,), (1,)), ((), ())), preferred_element_type=f32,
                ) * factor
                top = jnp.max(scores, axis=0, keepdims=True)
                weights = jnp.exp(scores - top)
                total = jnp.sum(weights, axis=0, keepdims=True)
                summed = lax.dot_general(
                    weights.astype(bf16), v_ref[block, :, cols],
                    (((0,), (0,)), ((), ())), preferred_element_type=f32,
                )
                scale = jnp.transpose(jnp.broadcast_to(1.0 / total, (LANES, LANES)))
                for h in range(together):
                    own = slice(h * count, (h + 1) * count)
                    piece = summed[own, h * HS:(h + 1) * HS] * scale[own]
                    out_ref[p, tokens, pl.ds((first + h) * HS, HS)] = piece.astype(bf16)
                lse = top + jnp.log(total)
                high = lse.astype(bf16).astype(f32)
                middle = (lse - high).astype(bf16).astype(f32)
                low = (lse - high - middle).astype(bf16).astype(f32)
                stat = jnp.where(
                    row == 0, high, jnp.where(row == 1, middle, jnp.where(row == 2, low, 0.0))
                )
                place = pl.ds((g * SLOTS + j) * LANES, LANES)
                out_ref[p, pl.ds(rows, STATS), place] = stat.astype(bf16)
        used = groups * SLOTS * LANES
        if used < width:
            rest = jnp.zeros((STATS, width - used), bf16)
            out_ref[p, pl.ds(rows, STATS), pl.ds(used, width - used)] = rest


def attend(ids, asked, keys, values):
    peer_count, given, width = asked.shape
    rows = SLOTS * (SPAN // PARTS)
    step = 4
    stored, tokens, _ = keys.shape
    slots = peer_count * SLOTS
    return pl.pallas_call(
        attend_kernel,
        out_shape=jax.ShapeDtypeStruct((peer_count, rows + STATS, width), bf16),
        grid_spec=pltpu.PrefetchScalarGridSpec(
            num_scalar_prefetch=1,
            grid=(peer_count // step,),
            in_specs=[
                pl.BlockSpec((step, given, width), lambda i, ids: (i, 0, 0)),
                pl.BlockSpec((stored, tokens, width), lambda i, ids: (0, 0, 0)),
                pl.BlockSpec((stored, tokens, width), lambda i, ids: (0, 0, 0)),
            ],
            out_specs=pl.BlockSpec((step, rows + STATS, width), lambda i, ids: (i, 0, 0)),
        ),
        compiler_params=pltpu.CompilerParams(dimension_semantics=("arbitrary",)),
        cost_estimate=pl.CostEstimate(
            flops=slots * 4 * LANES * LANES * width,
            bytes_accessed=4 * peer_count * rows * width,
            transcendentals=slots * LANES * LANES,
        ),
        name="attend",
    )(ids, asked, keys, values)


def combine_kernel(owner_ref, rank_ref, live_ref, back_ref, out_ref, part_ref, stat_ref, sems):
    spans, count, width = out_ref.shape
    together = LANES // count
    groups = width // HS // together
    rows = SLOTS * count
    copies = []
    for i in range(2 * spans):
        offset = pl.multiple_of(rank_ref[i] * count, count)
        source = back_ref.at[owner_ref[i]]
        copies.append((
            pltpu.make_async_copy(source.at[pl.ds(offset, count)], part_ref.at[i], sems.at[i, 0]),
            pltpu.make_async_copy(source.at[pl.ds(rows, STATS)], stat_ref.at[i], sems.at[i, 1]),
        ))
    for pair in copies:
        for copy in pair:
            copy.start()
    for s in range(spans):
        for n in range(2):
            for copy in copies[2 * s + n]:
                copy.wait()
        alive = s < live_ref[0]
        for g in range(groups):
            lses = []
            for n in range(2):
                start = pl.multiple_of((g * SLOTS + rank_ref[2 * s + n]) * LANES, LANES)
                stat = stat_ref[2 * s + n, :, pl.ds(start, LANES)].astype(f32)
                lses.append(stat[0:1] + stat[1:2] + stat[2:3])
            gap = lses[0] - lses[1]
            mine = jnp.transpose(jnp.broadcast_to(1.0 / (1.0 + jnp.exp(-gap)), (LANES, LANES)))
            other = jnp.transpose(jnp.broadcast_to(1.0 / (1.0 + jnp.exp(gap)), (LANES, LANES)))
            for h in range(together):
                own = slice(h * count, (h + 1) * count)
                cols = pl.ds((g * together + h) * HS, HS)
                merged = (
                    part_ref[2 * s, :, cols].astype(f32) * mine[own]
                    + part_ref[2 * s + 1, :, cols].astype(f32) * other[own]
                )
                out_ref[s, :, cols] = jnp.where(alive, merged, 0.0).astype(bf16)


def combine(owners, ranks, live, back):
    spans = owners.shape[0] // 2
    _, rows, width = back.shape
    count = (rows - STATS) // SLOTS
    smem = pl.BlockSpec(memory_space=pltpu.SMEM)
    return pl.pallas_call(
        combine_kernel,
        out_shape=jax.ShapeDtypeStruct((spans, count, width), bf16),
        in_specs=[smem, smem, smem, pl.BlockSpec(memory_space=pl.ANY)],
        out_specs=pl.BlockSpec(memory_space=pltpu.VMEM),
        scratch_shapes=[
            pltpu.VMEM((2 * spans, count, width), bf16),
            pltpu.VMEM((2 * spans, STATS, width), bf16),
            pltpu.SemaphoreType.DMA((2 * spans, 2)),
        ],
        cost_estimate=pl.CostEstimate(
            flops=8 * spans * count * width,
            bytes_accessed=6 * spans * count * width,
            transcendentals=0,
        ),
        name="combine",
    )(owners, ranks, live, back)


def shards(hidden, norm_gain, w_query, w_out, nb_keys, nb_values, neighbours, valid_spans):
    tok_rows, width = hidden.shape
    span_dev = tok_rows // SPAN
    stored = nb_keys.shape[0]
    inner_width = w_query.shape[1]
    peer_count = lax.axis_size("dp")
    count = SPAN // PARTS
    pieces = [
        hidden.reshape(span_dev, SPAN, width)[:, i * count:(i + 1) * count].reshape(-1, width)
        for i in range(PARTS)
    ]

    live_span = jnp.arange(span_dev, dtype=jnp.int32) < valid_spans[0]
    owners = (neighbours // stored).reshape(-1)
    slot_ids = (neighbours % stored).reshape(-1)
    is_live = jnp.repeat(live_span, 2)
    req_order = jnp.arange(owners.shape[0], dtype=jnp.int32)
    earlier = (
        (owners[:, None] == owners[None, :])
        & is_live[None, :]
        & (req_order[None, :] < req_order[:, None])
    )
    slot_rank = jnp.minimum(jnp.sum(earlier.astype(jnp.int32), axis=1), SLOTS - 1)
    target = jnp.where(is_live, owners * SLOTS + slot_rank, -1)
    slot_match = target[:, None] == jnp.arange(peer_count * SLOTS, dtype=jnp.int32)[None, :]
    request_table = jnp.sum(jnp.where(slot_match, slot_ids[:, None], 0), axis=0)
    source_span = jnp.sum(jnp.where(slot_match, req_order[:, None] // 2, 0), axis=0)
    def is_last(i):
        position = i * count + lax.broadcasted_iota(jnp.int32, (1, count, 1), 1)
        return position == SPAN - 1

    def request(i, piece):
        queries, nearly = project(piece, norm_gain, w_query)
        blocks = queries.reshape(span_dev, count, inner_width)
        following = shifted(blocks[:1], "dp", -1)
        turn = (i + 1) * count == SPAN
        return place(turn, i == 0, source_span, request_table, blocks, following), nearly

    def exchange(rows):
        return lax.all_to_all(rows, "dp", split_axis=0, concat_axis=0, tiled=True)

    def finish(i, back):
        merged = combine(owners, slot_rank, valid_spans, back)
        previous = shifted(merged[span_dev - 1 :], "dp", 1)
        placed = jnp.concatenate([previous, merged[: span_dev - 1]], axis=0)
        if (i + 1) * count == SPAN:
            placed = jnp.where(is_last(i), merged, placed)
        placed = placed.reshape(-1, inner_width)
        summed, late = output(placed, w_out)
        return summed.reshape(span_dev, count, width), late

    sent_0, nearly = request(0, pieces[0])
    piece_1, _ = lax.optimization_barrier((pieces[1], nearly))
    asked_0 = exchange(sent_0)
    sent_1, _ = request(1, piece_1)
    asked_0, sent_1 = lax.optimization_barrier((asked_0, sent_1))
    asked_1 = exchange(sent_1)
    wanted = asked_0[:, SLOTS * count, :SLOTS].astype(f32).astype(jnp.int32).reshape(-1)
    answers_0 = attend(wanted, asked_0, nb_keys, nb_values)
    back_0 = exchange(answers_0)
    answers_1 = attend(wanted, asked_1, nb_keys, nb_values)
    back_0, answers_1 = lax.optimization_barrier((back_0, answers_1))
    back_1 = exchange(answers_1)
    summed_0, late = finish(0, back_0)
    back_1, _ = lax.optimization_barrier((back_1, late))
    summed_1, _ = finish(1, back_1)
    summed = jnp.concatenate([summed_0, summed_1], axis=1)
    return hidden.astype(f32) + summed.reshape(tok_rows, width)


def solution(mesh):
    placed = (
        P("dp", "mp"),
        P(),
        P(None, "mp"),
        P("mp", None),
        P("dp", None, "mp"),
        P("dp", None, "mp"),
        P("dp", None),
        P("dp"),
    )
    return jax.shard_map(
        shards, mesh=mesh, in_specs=placed, out_specs=P("dp", "mp"), check_vma=False
    )
```

```python
import math

import jax
import jax.numpy as jnp
from jax import lax
from jax.experimental import pallas as pl
from jax.experimental.pallas import tpu as pltpu
from jax.sharding import PartitionSpec as P

HS = 128
SPAN = 64
SLOTS = 2
STATS = 8
PARTS = 1
LANES = 128

eps = 1e-05
f32 = jnp.float32
bf16 = jnp.bfloat16


def shifted(block, axis, distance):
    devices = range(lax.axis_size(axis))
    route = [(i - distance, i) for i in devices if i - distance in devices]
    return lax.ppermute(block, axis, route)


def turned(block, distance):
    size = lax.axis_size("mp")
    return lax.ppermute(block, "mp", [(i, (i + distance) % size) for i in range(size)])


def project(hidden, norm_gain, w_query):
    size = lax.axis_size("mp")
    me = lax.axis_index("mp")
    rows, width = hidden.shape
    half = rows // 2
    far = size // 2

    def weights(offset):
        start = (me + offset) % size * width
        gain = lax.dynamic_slice(norm_gain, (start,), (width,))
        part = lax.dynamic_slice(w_query, (start, 0), (width, w_query.shape[1]))
        return (part.astype(f32) * gain[:, None]).astype(bf16)

    def add(sums, h, block, weight):
        wide = block.astype(f32)
        squares = jnp.sum(wide * wide, axis=1, keepdims=True)
        product = jnp.dot(block, weight, preferred_element_type=f32)
        if sums[h] is None:
            sums[h] = (squares, product)
        else:
            sums[h] = (sums[h][0] + squares, sums[h][1] + product)

    sums = [None, None]
    up = [hidden[:half], hidden[half:]]
    down = list(up)
    own = weights(0)
    for step in range(1, far):
        behind, ahead = weights(-step), weights(step)
        for h in range(2):
            up[h] = turned(up[h], 1)
            down[1 - h] = turned(down[1 - h], -1)
        if step == 1:
            for h in range(2):
                mine = hidden[h * half:(h + 1) * half]
                mine, up[h] = lax.optimization_barrier((mine, up[h]))
                add(sums, h, mine, own)
        for h in range(2):
            add(sums, h, up[h], behind)
            add(sums, 1 - h, down[1 - h], ahead)
    opposite = weights(far)
    add(sums, 0, turned(up[0], 1), opposite)
    add(sums, 1, turned(down[1], -1), opposite)
    total = size * width
    return jnp.concatenate(
        [product * lax.rsqrt(squares / total + eps) for squares, product in sums], axis=0
    ).astype(bf16)


def output(halves, w_out):
    size = lax.axis_size("mp")
    me = lax.axis_index("mp")
    width = w_out.shape[1] // size
    far = size // 2

    def term(h, offset):
        start = (me + offset) % size * width
        part = lax.dynamic_slice(w_out, (0, start), (w_out.shape[0], width))
        return jnp.dot(halves[h], part, preferred_element_type=f32)

    arrived = {}
    for step in range(far):
        for h, way, offset in ((1, -1, far), (1, 1, far - 1), (0, 1, far), (0, -1, far - 1)):
            offset -= step
            if offset > 0:
                sums = term(h, way * offset)
                if (h, way) in arrived:
                    sums = sums + arrived[h, way].astype(f32)
                arrived[h, way] = turned(sums.astype(bf16), way)
    return jnp.concatenate(
        [term(h, 0) + arrived[h, 1].astype(f32) + arrived[h, -1].astype(f32) for h in range(2)], axis=0
    )


def attend_kernel(ids_ref, q_ref, k_ref, v_ref, out_ref):
    peers, rows, width = q_ref.shape
    count = rows // SLOTS
    together = LANES // count
    groups = width // HS // together
    step = pl.program_id(0)
    factor = 1.0 / math.sqrt(HS)
    zero = jnp.zeros((count, HS), bf16)
    row = lax.broadcasted_iota(jnp.int32, (STATS, LANES), 0)
    for p in range(peers):
        for j in range(SLOTS):
            block = ids_ref[(step * peers + p) * SLOTS + j]
            tokens = pl.ds(j * count, count)
            for g in range(groups):
                first = g * together
                cols = pl.ds(first * HS, together * HS)
                spread = []
                for h in range(together):
                    line = [zero] * together
                    line[h] = q_ref[p, tokens, pl.ds((first + h) * HS, HS)]
                    spread.append(jnp.concatenate(line, axis=1))
                scores = lax.dot_general(
                    k_ref[block, :, cols], jnp.concatenate(spread, axis=0),
                    (((1,), (1,)), ((), ())), preferred_element_type=f32,
                ) * factor
                top = jnp.max(scores, axis=0, keepdims=True)
                weights = jnp.exp(scores - top)
                total = jnp.sum(weights, axis=0, keepdims=True)
                summed = lax.dot_general(
                    weights.astype(bf16), v_ref[block, :, cols],
                    (((0,), (0,)), ((), ())), preferred_element_type=f32,
                )
                scale = jnp.transpose(jnp.broadcast_to(1.0 / total, (LANES, LANES)))
                for h in range(together):
                    own = slice(h * count, (h + 1) * count)
                    piece = summed[own, h * HS:(h + 1) * HS] * scale[own]
                    out_ref[p, tokens, pl.ds((first + h) * HS, HS)] = piece.astype(bf16)
                lse = top + jnp.log(total)
                high = lse.astype(bf16).astype(f32)
                middle = (lse - high).astype(bf16).astype(f32)
                low = (lse - high - middle).astype(bf16).astype(f32)
                stat = jnp.where(
                    row == 0, high, jnp.where(row == 1, middle, jnp.where(row == 2, low, 0.0))
                )
                place = pl.ds((g * SLOTS + j) * LANES, LANES)
                out_ref[p, pl.ds(rows, STATS), place] = stat.astype(bf16)
        used = groups * SLOTS * LANES
        if used < width:
            rest = jnp.zeros((STATS, width - used), bf16)
            out_ref[p, pl.ds(rows, STATS), pl.ds(used, width - used)] = rest


def attend(ids, asked, keys, values):
    peer_count, rows, width = asked.shape
    step = 8
    stored, tokens, _ = keys.shape
    slots = peer_count * SLOTS
    return pl.pallas_call(
        attend_kernel,
        out_shape=jax.ShapeDtypeStruct((peer_count, rows + STATS, width), bf16),
        grid_spec=pltpu.PrefetchScalarGridSpec(
            num_scalar_prefetch=1,
            grid=(peer_count // step,),
            in_specs=[
                pl.BlockSpec((step, rows, width), lambda i, ids: (i, 0, 0)),
                pl.BlockSpec((stored, tokens, width), lambda i, ids: (0, 0, 0)),
                pl.BlockSpec((stored, tokens, width), lambda i, ids: (0, 0, 0)),
            ],
            out_specs=pl.BlockSpec((step, rows + STATS, width), lambda i, ids: (i, 0, 0)),
        ),
        compiler_params=pltpu.CompilerParams(dimension_semantics=("arbitrary",)),
        cost_estimate=pl.CostEstimate(
            flops=slots * 4 * LANES * LANES * width,
            bytes_accessed=4 * peer_count * rows * width,
            transcendentals=slots * LANES * LANES,
        ),
        name="attend",
    )(ids, asked, keys, values)


def combine_kernel(
    owner_ref, rank_ref, live_ref, back_ref, low_ref, high_ref, tail_ref, part_ref, stat_ref, sems
):
    spans, count, width = part_ref.shape
    spans //= 2
    together = LANES // count
    groups = width // HS // together
    rows = SLOTS * count
    copies = []
    for i in range(2 * spans):
        offset = pl.multiple_of(rank_ref[i] * count, count)
        source = back_ref.at[owner_ref[i]]
        copies.append((
            pltpu.make_async_copy(source.at[pl.ds(offset, count)], part_ref.at[i], sems.at[i, 0]),
            pltpu.make_async_copy(source.at[pl.ds(rows, STATS)], stat_ref.at[i], sems.at[i, 1]),
        ))
    for pair in copies:
        for copy in pair:
            copy.start()
    is_last = lax.broadcasted_iota(jnp.int32, (count, HS), 0) == count - 1
    before = [jnp.zeros((count, HS), f32)] * (width // HS)
    for s in range(spans):
        for n in range(2):
            for copy in copies[2 * s + n]:
                copy.wait()
        alive = s < live_ref[0]
        block_ref = low_ref.at[s] if s < spans // 2 else high_ref.at[s - spans // 2]
        for g in range(groups):
            lses = []
            for n in range(2):
                start = pl.multiple_of((g * SLOTS + rank_ref[2 * s + n]) * LANES, LANES)
                stat = stat_ref[2 * s + n, :, pl.ds(start, LANES)].astype(f32)
                lses.append(stat[0:1] + stat[1:2] + stat[2:3])
            gap = lses[0] - lses[1]
            mine = jnp.transpose(jnp.broadcast_to(1.0 / (1.0 + jnp.exp(-gap)), (LANES, LANES)))
            other = jnp.transpose(jnp.broadcast_to(1.0 / (1.0 + jnp.exp(gap)), (LANES, LANES)))
            for h in range(together):
                own = slice(h * count, (h + 1) * count)
                head = g * together + h
                cols = pl.ds(head * HS, HS)
                merged = (
                    part_ref[2 * s, :, cols].astype(f32) * mine[own]
                    + part_ref[2 * s + 1, :, cols].astype(f32) * other[own]
                )
                merged = jnp.where(alive, merged, 0.0)
                block_ref[:, cols] = jnp.where(is_last, merged, before[head]).astype(bf16)
                before[head] = merged
                if s == spans - 1:
                    tail_ref[:, cols] = merged.astype(bf16)


def combine(owners, ranks, live, back):
    spans = owners.shape[0] // 2
    _, rows, width = back.shape
    count = (rows - STATS) // SLOTS
    smem = pl.BlockSpec(memory_space=pltpu.SMEM)
    vmem = pl.BlockSpec(memory_space=pltpu.VMEM)
    half = jax.ShapeDtypeStruct((spans // 2, count, width), bf16)
    return pl.pallas_call(
        combine_kernel,
        out_shape=[half, half, jax.ShapeDtypeStruct((count, width), bf16)],
        in_specs=[smem, smem, smem, pl.BlockSpec(memory_space=pl.ANY)],
        out_specs=[vmem, vmem, vmem],
        scratch_shapes=[
            pltpu.VMEM((2 * spans, count, width), bf16),
            pltpu.VMEM((2 * spans, STATS, width), bf16),
            pltpu.SemaphoreType.DMA((2 * spans, 2)),
        ],
        cost_estimate=pl.CostEstimate(
            flops=8 * spans * count * width,
            bytes_accessed=6 * spans * count * width,
            transcendentals=0,
        ),
        name="combine",
    )(owners, ranks, live, back)


def shards(hidden, norm_gain, w_query, w_out, nb_keys, nb_values, neighbours, valid_spans):
    tok_rows, width = hidden.shape
    span_dev = tok_rows // SPAN
    stored = nb_keys.shape[0]
    inner_width = w_query.shape[1]
    peer_count = lax.axis_size("dp")
    count = SPAN // PARTS
    live_span = jnp.arange(span_dev, dtype=jnp.int32) < valid_spans[0]
    owners = (neighbours // stored).reshape(-1)
    slot_ids = (neighbours % stored).reshape(-1)
    is_live = jnp.repeat(live_span, 2)
    req_order = jnp.arange(owners.shape[0], dtype=jnp.int32)
    earlier = (
        (owners[:, None] == owners[None, :])
        & is_live[None, :]
        & (req_order[None, :] < req_order[:, None])
    )
    slot_rank = jnp.minimum(jnp.sum(earlier.astype(jnp.int32), axis=1), SLOTS - 1)
    target = jnp.where(is_live, owners * SLOTS + slot_rank, -1)
    slot_match = target[:, None] == jnp.arange(peer_count * SLOTS, dtype=jnp.int32)[None, :]
    request_table = jnp.sum(jnp.where(slot_match, slot_ids[:, None], 0), axis=0)
    request_table = request_table.reshape(peer_count, SLOTS)
    source_span = jnp.sum(jnp.where(slot_match, req_order[:, None] // 2, 0), axis=0)
    wanted = lax.all_to_all(request_table, "dp", split_axis=0, concat_axis=0, tiled=True)
    wanted = wanted.reshape(-1)

    def is_last(i):
        position = i * count + lax.broadcasted_iota(jnp.int32, (1, count, 1), 1)
        return position == SPAN - 1

    def ask(i):
        queries = project(hidden, norm_gain, w_query)
        blocks = queries.reshape(span_dev, count, inner_width)
        following = shifted(blocks[:1], "dp", -1)
        grouped = jnp.concatenate([blocks[1:], following], axis=0)
        if (i + 1) * count == SPAN:
            grouped = jnp.where(is_last(i), blocks, grouped)
        sent_rows = grouped[source_span].reshape(peer_count, SLOTS * count, inner_width)
        return lax.all_to_all(sent_rows, "dp", split_axis=0, concat_axis=0, tiled=True)

    def answer(asked):
        answers = attend(wanted, asked, nb_keys, nb_values)
        return lax.all_to_all(answers, "dp", split_axis=0, concat_axis=0, tiled=True)

    def finish(i, back):
        low, high, tail = combine(owners, slot_rank, valid_spans, back)
        previous = shifted(tail, "dp", 1)
        low = low.reshape(-1, inner_width)
        row = lax.broadcasted_iota(jnp.int32, (low.shape[0], 1), 0)
        previous = jnp.pad(previous, ((0, low.shape[0] - SPAN), (0, 0)))
        low = jnp.where(row < SPAN - 1, previous, low)
        return output([low, high.reshape(-1, inner_width)], w_out).reshape(span_dev, count, width)

    asked = [ask(i) for i in range(PARTS)]
    back = [answer(one) for one in asked]
    summed = [finish(i, one) for i, one in enumerate(back)]
    summed = jnp.concatenate(summed, axis=1).reshape(tok_rows, width)
    return hidden.astype(f32) + summed


def solution(mesh):
    placed = (
        P("dp", "mp"),
        P(),
        P(None, "mp"),
        P("mp", None),
        P("dp", None, "mp"),
        P("dp", None, "mp"),
        P("dp", None),
        P("dp"),
    )
    return jax.shard_map(
        shards, mesh=mesh, in_specs=placed, out_specs=P("dp", "mp"), check_vma=False
    )
```

```python
import math

import jax
import jax.numpy as jnp
from jax import lax
from jax.experimental import pallas as pl
from jax.experimental.pallas import tpu as pltpu
from jax.sharding import PartitionSpec as P

HS = 128
SPAN = 64
SLOTS = 2
STATS = 8
PARTS = 1
LANES = 128

eps = 1e-05
f32 = jnp.float32
bf16 = jnp.bfloat16


def shifted(block, axis, distance):
    devices = range(lax.axis_size(axis))
    route = [(i - distance, i) for i in devices if i - distance in devices]
    return lax.ppermute(block, axis, route)


def turned(block, distance):
    size = lax.axis_size("mp")
    return lax.ppermute(block, "mp", [(i, (i + distance) % size) for i in range(size)])


def project(hidden, norm_gain, w_query):
    size = lax.axis_size("mp")
    me = lax.axis_index("mp")
    rows, width = hidden.shape
    half = rows // 2
    far = size // 2

    def weights(offset):
        start = (me + offset) % size * width
        gain = lax.dynamic_slice(norm_gain, (start,), (width,))
        part = lax.dynamic_slice(w_query, (start, 0), (width, w_query.shape[1]))
        return (part.astype(f32) * gain[:, None]).astype(bf16)

    def add(sums, h, block, weight):
        wide = block.astype(f32)
        squares = jnp.sum(wide * wide, axis=1, keepdims=True)
        product = jnp.dot(block, weight, preferred_element_type=f32)
        if sums[h] is None:
            sums[h] = (squares, product)
        else:
            sums[h] = (sums[h][0] + squares, sums[h][1] + product)

    sums = [None, None]
    up = [hidden[:half], hidden[half:]]
    down = list(up)
    own = weights(0)
    for step in range(1, far):
        behind, ahead = weights(-step), weights(step)
        for h in range(2):
            up[h] = turned(up[h], 1)
            down[1 - h] = turned(down[1 - h], -1)
        if step == 1:
            for h in range(2):
                mine = hidden[h * half:(h + 1) * half]
                mine, up[h] = lax.optimization_barrier((mine, up[h]))
                add(sums, h, mine, own)
        for h in range(2):
            add(sums, h, up[h], behind)
            add(sums, 1 - h, down[1 - h], ahead)
    opposite = weights(far)
    add(sums, 0, turned(up[0], 1), opposite)
    add(sums, 1, turned(down[1], -1), opposite)
    total = size * width
    return jnp.concatenate(
        [product * lax.rsqrt(squares / total + eps) for squares, product in sums], axis=0
    ).astype(bf16)


def output(halves, w_out):
    size = lax.axis_size("mp")
    me = lax.axis_index("mp")
    width = w_out.shape[1] // size
    far = size // 2

    def term(h, offset):
        start = (me + offset) % size * width
        part = lax.dynamic_slice(w_out, (0, start), (w_out.shape[0], width))
        return jnp.dot(halves[h], part, preferred_element_type=f32)

    arrived = {}
    for step in range(far):
        new = {}
        for h, way, offset in ((1, -1, far), (1, 1, far - 1), (0, 1, far), (0, -1, far - 1)):
            offset -= step
            new[h, way] = offset > 0
            if offset > 0:
                sums = term(h, way * offset)
                if (h, way) in arrived:
                    sums = sums + arrived[h, way].astype(f32)
                arrived[h, way] = sums.astype(bf16)
        if step == 0:
            for h in range(2):
                arrived[h, 1], arrived[h, -1], halves[h] = lax.optimization_barrier(
                    (arrived[h, 1], arrived[h, -1], halves[h])
                )
        arrived = {(h, way): turned(sums, way) if new[h, way] else sums for (h, way), sums in arrived.items()}
    return jnp.concatenate(
        [term(h, 0) + arrived[h, 1].astype(f32) + arrived[h, -1].astype(f32) for h in range(2)], axis=0
    )


def attend_kernel(ids_ref, q_ref, k_ref, v_ref, out_ref):
    peers, rows, width = q_ref.shape
    count = rows // SLOTS
    together = LANES // count
    groups = width // HS // together
    step = pl.program_id(0)
    factor = 1.0 / math.sqrt(HS)
    zero = jnp.zeros((count, HS), bf16)
    row = lax.broadcasted_iota(jnp.int32, (STATS, LANES), 0)
    for p in range(peers):
        for j in range(SLOTS):
            block = ids_ref[(step * peers + p) * SLOTS + j]
            tokens = pl.ds(j * count, count)
            for g in range(groups):
                first = g * together
                cols = pl.ds(first * HS, together * HS)
                spread = []
                for h in range(together):
                    line = [zero] * together
                    line[h] = q_ref[p, tokens, pl.ds((first + h) * HS, HS)]
                    spread.append(jnp.concatenate(line, axis=1))
                scores = lax.dot_general(
                    k_ref[block, :, cols], jnp.concatenate(spread, axis=0),
                    (((1,), (1,)), ((), ())), preferred_element_type=f32,
                ) * factor
                top = jnp.max(scores, axis=0, keepdims=True)
                weights = jnp.exp(scores - top)
                total = jnp.sum(weights, axis=0, keepdims=True)
                summed = lax.dot_general(
                    weights.astype(bf16), v_ref[block, :, cols],
                    (((0,), (0,)), ((), ())), preferred_element_type=f32,
                )
                scale = jnp.transpose(jnp.broadcast_to(1.0 / total, (LANES, LANES)))
                for h in range(together):
                    own = slice(h * count, (h + 1) * count)
                    piece = summed[own, h * HS:(h + 1) * HS] * scale[own]
                    out_ref[p, tokens, pl.ds((first + h) * HS, HS)] = piece.astype(bf16)
                lse = top + jnp.log(total)
                high = lse.astype(bf16).astype(f32)
                middle = (lse - high).astype(bf16).astype(f32)
                low = (lse - high - middle).astype(bf16).astype(f32)
                stat = jnp.where(
                    row == 0, high, jnp.where(row == 1, middle, jnp.where(row == 2, low, 0.0))
                )
                place = pl.ds((g * SLOTS + j) * LANES, LANES)
                out_ref[p, pl.ds(rows, STATS), place] = stat.astype(bf16)
        used = groups * SLOTS * LANES
        if used < width:
            rest = jnp.zeros((STATS, width - used), bf16)
            out_ref[p, pl.ds(rows, STATS), pl.ds(used, width - used)] = rest


def attend(ids, asked, keys, values):
    peer_count, rows, width = asked.shape
    step = 8
    stored, tokens, _ = keys.shape
    slots = peer_count * SLOTS
    return pl.pallas_call(
        attend_kernel,
        out_shape=jax.ShapeDtypeStruct((peer_count, rows + STATS, width), bf16),
        grid_spec=pltpu.PrefetchScalarGridSpec(
            num_scalar_prefetch=1,
            grid=(peer_count // step,),
            in_specs=[
                pl.BlockSpec((step, rows, width), lambda i, ids: (i, 0, 0)),
                pl.BlockSpec((stored, tokens, width), lambda i, ids: (0, 0, 0)),
                pl.BlockSpec((stored, tokens, width), lambda i, ids: (0, 0, 0)),
            ],
            out_specs=pl.BlockSpec((step, rows + STATS, width), lambda i, ids: (i, 0, 0)),
        ),
        compiler_params=pltpu.CompilerParams(dimension_semantics=("arbitrary",)),
        cost_estimate=pl.CostEstimate(
            flops=slots * 4 * LANES * LANES * width,
            bytes_accessed=4 * peer_count * rows * width,
            transcendentals=slots * LANES * LANES,
        ),
        name="attend",
    )(ids, asked, keys, values)


def combine_kernel(
    owner_ref, rank_ref, live_ref, back_ref, low_ref, high_ref, tail_ref, part_ref, stat_ref, sems
):
    spans, count, width = part_ref.shape
    spans //= 2
    together = LANES // count
    groups = width // HS // together
    rows = SLOTS * count
    copies = []
    for i in range(2 * spans):
        offset = pl.multiple_of(rank_ref[i] * count, count)
        source = back_ref.at[owner_ref[i]]
        copies.append((
            pltpu.make_async_copy(source.at[pl.ds(offset, count)], part_ref.at[i], sems.at[i, 0]),
            pltpu.make_async_copy(source.at[pl.ds(rows, STATS)], stat_ref.at[i], sems.at[i, 1]),
        ))
    for pair in copies:
        for copy in pair:
            copy.start()
    is_last = lax.broadcasted_iota(jnp.int32, (count, HS), 0) == count - 1
    before = [jnp.zeros((count, HS), f32)] * (width // HS)
    for s in range(spans):
        for n in range(2):
            for copy in copies[2 * s + n]:
                copy.wait()
        alive = s < live_ref[0]
        block_ref = low_ref.at[s] if s < spans // 2 else high_ref.at[s - spans // 2]
        for g in range(groups):
            lses = []
            for n in range(2):
                start = pl.multiple_of((g * SLOTS + rank_ref[2 * s + n]) * LANES, LANES)
                stat = stat_ref[2 * s + n, :, pl.ds(start, LANES)].astype(f32)
                lses.append(stat[0:1] + stat[1:2] + stat[2:3])
            gap = lses[0] - lses[1]
            mine = jnp.transpose(jnp.broadcast_to(1.0 / (1.0 + jnp.exp(-gap)), (LANES, LANES)))
            other = jnp.transpose(jnp.broadcast_to(1.0 / (1.0 + jnp.exp(gap)), (LANES, LANES)))
            for h in range(together):
                own = slice(h * count, (h + 1) * count)
                head = g * together + h
                cols = pl.ds(head * HS, HS)
                merged = (
                    part_ref[2 * s, :, cols].astype(f32) * mine[own]
                    + part_ref[2 * s + 1, :, cols].astype(f32) * other[own]
                )
                merged = jnp.where(alive, merged, 0.0)
                block_ref[:, cols] = jnp.where(is_last, merged, before[head]).astype(bf16)
                before[head] = merged
                if s == spans - 1:
                    tail_ref[:, cols] = merged.astype(bf16)


def combine(owners, ranks, live, back):
    spans = owners.shape[0] // 2
    _, rows, width = back.shape
    count = (rows - STATS) // SLOTS
    smem = pl.BlockSpec(memory_space=pltpu.SMEM)
    vmem = pl.BlockSpec(memory_space=pltpu.VMEM)
    half = jax.ShapeDtypeStruct((spans // 2, count, width), bf16)
    return pl.pallas_call(
        combine_kernel,
        out_shape=[half, half, jax.ShapeDtypeStruct((count, width), bf16)],
        in_specs=[smem, smem, smem, pl.BlockSpec(memory_space=pl.ANY)],
        out_specs=[vmem, vmem, vmem],
        scratch_shapes=[
            pltpu.VMEM((2 * spans, count, width), bf16),
            pltpu.VMEM((2 * spans, STATS, width), bf16),
            pltpu.SemaphoreType.DMA((2 * spans, 2)),
        ],
        cost_estimate=pl.CostEstimate(
            flops=8 * spans * count * width,
            bytes_accessed=6 * spans * count * width,
            transcendentals=0,
        ),
        name="combine",
    )(owners, ranks, live, back)


def shards(hidden, norm_gain, w_query, w_out, nb_keys, nb_values, neighbours, valid_spans):
    tok_rows, width = hidden.shape
    span_dev = tok_rows // SPAN
    stored = nb_keys.shape[0]
    inner_width = w_query.shape[1]
    peer_count = lax.axis_size("dp")
    count = SPAN // PARTS
    live_span = jnp.arange(span_dev, dtype=jnp.int32) < valid_spans[0]
    owners = (neighbours // stored).reshape(-1)
    slot_ids = (neighbours % stored).reshape(-1)
    is_live = jnp.repeat(live_span, 2)
    req_order = jnp.arange(owners.shape[0], dtype=jnp.int32)
    earlier = (
        (owners[:, None] == owners[None, :])
        & is_live[None, :]
        & (req_order[None, :] < req_order[:, None])
    )
    slot_rank = jnp.minimum(jnp.sum(earlier.astype(jnp.int32), axis=1), SLOTS - 1)
    target = jnp.where(is_live, owners * SLOTS + slot_rank, -1)
    slot_match = target[:, None] == jnp.arange(peer_count * SLOTS, dtype=jnp.int32)[None, :]
    source_span = jnp.sum(jnp.where(slot_match, req_order[:, None] // 2, 0), axis=0)
    named = jnp.where(is_live, neighbours.reshape(-1), -1)[None, :]

    def wanted_blocks(table):
        me = lax.axis_index("dp")
        while table.shape[0] < peer_count:
            step = table.shape[0]
            route = [(i, (i - step) % peer_count) for i in range(peer_count)]
            table = jnp.concatenate([table, lax.ppermute(table, "dp", route)], axis=0)
        mine = (table >= 0) & (table // stored == me)
        before = req_order[None, None, :] < req_order[None, :, None]
        rank = jnp.sum((mine[:, None, :] & before).astype(jnp.int32), axis=2)
        block = jnp.where(mine, table % stored, 0)
        found = [jnp.sum(jnp.where(rank == k, block, 0), axis=1) for k in range(SLOTS)]
        peers = jnp.arange(peer_count, dtype=jnp.int32)
        turn = (peers[None, :] + me) % peer_count == peers[:, None]
        return jnp.stack(
            [jnp.sum(jnp.where(turn, one[None, :], 0), axis=1) for one in found], axis=1
        ).reshape(-1)

    def is_last(i):
        position = i * count + lax.broadcasted_iota(jnp.int32, (1, count, 1), 1)
        return position == SPAN - 1

    def ask(i):
        queries = project(hidden, norm_gain, w_query)
        blocks = queries.reshape(span_dev, count, inner_width)
        following = shifted(blocks[:1], "dp", -1)
        grouped = jnp.concatenate([blocks[1:], following], axis=0)
        if (i + 1) * count == SPAN:
            grouped = jnp.where(is_last(i), blocks, grouped)
        sent_rows = grouped[source_span].reshape(peer_count, SLOTS * count, inner_width)
        sent_rows, table = lax.optimization_barrier((sent_rows, named))
        asked = lax.all_to_all(sent_rows, "dp", split_axis=0, concat_axis=0, tiled=True)
        return asked, wanted_blocks(table)

    def answer(request):
        asked, wanted = request
        answers = attend(wanted, asked, nb_keys, nb_values)
        return lax.all_to_all(answers, "dp", split_axis=0, concat_axis=0, tiled=True)

    def finish(i, back):
        low, high, tail = combine(owners, slot_rank, valid_spans, back)
        previous = shifted(tail, "dp", 1)
        low = low.reshape(-1, inner_width)
        row = lax.broadcasted_iota(jnp.int32, (low.shape[0], 1), 0)
        previous = jnp.pad(previous, ((0, low.shape[0] - SPAN), (0, 0)))
        low = jnp.where(row < SPAN - 1, previous, low)
        return output([low, high.reshape(-1, inner_width)], w_out).reshape(span_dev, count, width)

    asked = [ask(i) for i in range(PARTS)]
    back = [answer(one) for one in asked]
    summed = [finish(i, one) for i, one in enumerate(back)]
    summed = jnp.concatenate(summed, axis=1).reshape(tok_rows, width)
    return hidden.astype(f32) + summed


def solution(mesh):
    placed = (
        P("dp", "mp"),
        P(),
        P(None, "mp"),
        P("mp", None),
        P("dp", None, "mp"),
        P("dp", None, "mp"),
        P("dp", None),
        P("dp"),
    )
    return jax.shard_map(
        shards, mesh=mesh, in_specs=placed, out_specs=P("dp", "mp"), check_vma=False
    )
```

```python
import math

import jax
import jax.numpy as jnp
from jax import lax
from jax.experimental import pallas as pl
from jax.experimental.pallas import tpu as pltpu
from jax.sharding import PartitionSpec as P

HS = 128
SPAN = 64
SLOTS = 2
STATS = 8
PARTS = 1
LANES = 128

eps = 1e-05
f32 = jnp.float32
bf16 = jnp.bfloat16


def shifted(block, axis, distance):
    devices = range(lax.axis_size(axis))
    route = [(i - distance, i) for i in devices if i - distance in devices]
    return lax.ppermute(block, axis, route)


def turned(block, distance):
    size = lax.axis_size("mp")
    return lax.ppermute(block, "mp", [(i, (i + distance) % size) for i in range(size)])


def project(hidden, norm_gain, w_query):
    size = lax.axis_size("mp")
    me = lax.axis_index("mp")
    rows, width = hidden.shape
    half = rows // 2
    far = size // 2

    def weights(offset):
        start = (me + offset) % size * width
        gain = lax.dynamic_slice(norm_gain, (start,), (width,))
        part = lax.dynamic_slice(w_query, (start, 0), (width, w_query.shape[1]))
        return (part.astype(f32) * gain[:, None]).astype(bf16)

    def add(sums, h, block, weight):
        wide = block.astype(f32)
        squares = jnp.sum(wide * wide, axis=1, keepdims=True)
        product = jnp.dot(block, weight, preferred_element_type=f32)
        if sums[h] is None:
            sums[h] = (squares, product)
        else:
            sums[h] = (sums[h][0] + squares, sums[h][1] + product)

    sums = [None, None]
    up = [hidden[:half], hidden[half:]]
    down = list(up)
    own = weights(0)
    for step in range(1, far):
        behind, ahead = weights(-step), weights(step)
        for h in range(2):
            up[h] = turned(up[h], 1)
            down[1 - h] = turned(down[1 - h], -1)
        if step == 1:
            for h in range(2):
                mine = hidden[h * half:(h + 1) * half]
                mine, up[h] = lax.optimization_barrier((mine, up[h]))
                add(sums, h, mine, own)
        for h in range(2):
            add(sums, h, up[h], behind)
            add(sums, 1 - h, down[1 - h], ahead)
    opposite = weights(far)
    add(sums, 0, turned(up[0], 1), opposite)
    add(sums, 1, turned(down[1], -1), opposite)
    total = size * width
    return jnp.concatenate(
        [product * lax.rsqrt(squares / total + eps) for squares, product in sums], axis=0
    ).astype(bf16)


def output(halves, w_out):
    size = lax.axis_size("mp")
    me = lax.axis_index("mp")
    width = w_out.shape[1] // size
    far = size // 2

    def term(h, offset):
        start = (me + offset) % size * width
        part = lax.dynamic_slice(w_out, (0, start), (w_out.shape[0], width))
        return jnp.dot(halves[h], part, preferred_element_type=f32)

    arrived = {}
    for step in range(far):
        new = {}
        for h, way, offset in ((1, -1, far), (1, 1, far - 1), (0, 1, far), (0, -1, far - 1)):
            offset -= step
            new[h, way] = offset > 0
            if offset > 0:
                sums = term(h, way * offset)
                if (h, way) in arrived:
                    sums = sums + arrived[h, way].astype(f32)
                arrived[h, way] = sums.astype(bf16)
        if step == 0:
            for h in range(2):
                arrived[h, 1], arrived[h, -1], halves[h] = lax.optimization_barrier(
                    (arrived[h, 1], arrived[h, -1], halves[h])
                )
        arrived = {(h, way): turned(sums, way) if new[h, way] else sums for (h, way), sums in arrived.items()}
    return jnp.concatenate(
        [term(h, 0) + arrived[h, 1].astype(f32) + arrived[h, -1].astype(f32) for h in range(2)], axis=0
    )


def attend_kernel(ids_ref, q_ref, k_ref, v_ref, out_ref):
    peers, rows, width = q_ref.shape
    count = rows // SLOTS
    together = LANES // count
    groups = width // HS // together
    step = pl.program_id(0)
    factor = 1.0 / math.sqrt(HS)
    zero = jnp.zeros((count, HS), bf16)
    row = lax.broadcasted_iota(jnp.int32, (STATS, LANES), 0)
    for p in range(peers):
        for j in range(SLOTS):
            block = ids_ref[(step * peers + p) * SLOTS + j]
            tokens = pl.ds(j * count, count)
            for g in range(groups):
                first = g * together
                cols = pl.ds(first * HS, together * HS)
                spread = []
                for h in range(together):
                    line = [zero] * together
                    line[h] = q_ref[p, tokens, pl.ds((first + h) * HS, HS)]
                    spread.append(jnp.concatenate(line, axis=1))
                scores = lax.dot_general(
                    k_ref[block, :, cols], jnp.concatenate(spread, axis=0),
                    (((1,), (1,)), ((), ())), preferred_element_type=f32,
                ) * factor
                top = jnp.max(scores, axis=0, keepdims=True)
                weights = jnp.exp(scores - top)
                total = jnp.sum(weights, axis=0, keepdims=True)
                summed = lax.dot_general(
                    weights.astype(bf16), v_ref[block, :, cols],
                    (((0,), (0,)), ((), ())), preferred_element_type=f32,
                )
                scale = jnp.transpose(jnp.broadcast_to(1.0 / total, (LANES, LANES)))
                for h in range(together):
                    own = slice(h * count, (h + 1) * count)
                    piece = summed[own, h * HS:(h + 1) * HS] * scale[own]
                    out_ref[p, tokens, pl.ds((first + h) * HS, HS)] = piece.astype(bf16)
                lse = top + jnp.log(total)
                high = lse.astype(bf16).astype(f32)
                middle = (lse - high).astype(bf16).astype(f32)
                low = (lse - high - middle).astype(bf16).astype(f32)
                stat = jnp.where(
                    row == 0, high, jnp.where(row == 1, middle, jnp.where(row == 2, low, 0.0))
                )
                place = pl.ds((g * SLOTS + j) * LANES, LANES)
                out_ref[p, pl.ds(rows, STATS), place] = stat.astype(bf16)
        used = groups * SLOTS * LANES
        if used < width:
            rest = jnp.zeros((STATS, width - used), bf16)
            out_ref[p, pl.ds(rows, STATS), pl.ds(used, width - used)] = rest


def attend(ids, asked, keys, values):
    peer_count, rows, width = asked.shape
    step = 8
    stored, tokens, _ = keys.shape
    slots = peer_count * SLOTS
    return pl.pallas_call(
        attend_kernel,
        out_shape=jax.ShapeDtypeStruct((peer_count, rows + STATS, width), bf16),
        grid_spec=pltpu.PrefetchScalarGridSpec(
            num_scalar_prefetch=1,
            grid=(peer_count // step,),
            in_specs=[
                pl.BlockSpec((step, rows, width), lambda i, ids: (i, 0, 0)),
                pl.BlockSpec((stored, tokens, width), lambda i, ids: (0, 0, 0)),
                pl.BlockSpec((stored, tokens, width), lambda i, ids: (0, 0, 0)),
            ],
            out_specs=pl.BlockSpec((step, rows + STATS, width), lambda i, ids: (i, 0, 0)),
        ),
        compiler_params=pltpu.CompilerParams(dimension_semantics=("arbitrary",)),
        cost_estimate=pl.CostEstimate(
            flops=slots * 4 * LANES * LANES * width,
            bytes_accessed=4 * peer_count * rows * width,
            transcendentals=slots * LANES * LANES,
        ),
        name="attend",
    )(ids, asked, keys, values)


def combine_kernel(
    owner_ref, rank_ref, live_ref, back_ref, low_ref, high_ref, tail_ref, part_ref, stat_ref, sems
):
    spans, count, width = part_ref.shape
    spans //= 2
    together = LANES // count
    groups = width // HS // together
    rows = SLOTS * count
    copies = []
    for i in range(2 * spans):
        offset = pl.multiple_of(rank_ref[i] * count, count)
        source = back_ref.at[owner_ref[i]]
        copies.append((
            pltpu.make_async_copy(source.at[pl.ds(offset, count)], part_ref.at[i], sems.at[i, 0]),
            pltpu.make_async_copy(source.at[pl.ds(rows, STATS)], stat_ref.at[i], sems.at[i, 1]),
        ))
    for pair in copies:
        for copy in pair:
            copy.start()
    is_last = lax.broadcasted_iota(jnp.int32, (count, HS), 0) == count - 1
    before = [jnp.zeros((count, HS), f32)] * (width // HS)
    for s in range(spans):
        for n in range(2):
            for copy in copies[2 * s + n]:
                copy.wait()
        alive = s < live_ref[0]
        block_ref = low_ref.at[s] if s < spans // 2 else high_ref.at[s - spans // 2]
        for g in range(groups):
            lses = []
            for n in range(2):
                start = pl.multiple_of((g * SLOTS + rank_ref[2 * s + n]) * LANES, LANES)
                stat = stat_ref[2 * s + n, :, pl.ds(start, LANES)].astype(f32)
                lses.append(stat[0:1] + stat[1:2] + stat[2:3])
            gap = lses[0] - lses[1]
            mine = jnp.transpose(jnp.broadcast_to(1.0 / (1.0 + jnp.exp(-gap)), (LANES, LANES)))
            other = jnp.transpose(jnp.broadcast_to(1.0 / (1.0 + jnp.exp(gap)), (LANES, LANES)))
            for h in range(together):
                own = slice(h * count, (h + 1) * count)
                head = g * together + h
                cols = pl.ds(head * HS, HS)
                merged = (
                    part_ref[2 * s, :, cols].astype(f32) * mine[own]
                    + part_ref[2 * s + 1, :, cols].astype(f32) * other[own]
                )
                merged = jnp.where(alive, merged, 0.0)
                block_ref[:, cols] = jnp.where(is_last, merged, before[head]).astype(bf16)
                before[head] = merged
                if s == spans - 1:
                    tail_ref[:, cols] = merged.astype(bf16)


def combine(owners, ranks, live, back):
    spans = owners.shape[0] // 2
    _, rows, width = back.shape
    count = (rows - STATS) // SLOTS
    smem = pl.BlockSpec(memory_space=pltpu.SMEM)
    vmem = pl.BlockSpec(memory_space=pltpu.VMEM)
    half = jax.ShapeDtypeStruct((spans // 2, count, width), bf16)
    return pl.pallas_call(
        combine_kernel,
        out_shape=[half, half, jax.ShapeDtypeStruct((count, width), bf16)],
        in_specs=[smem, smem, smem, pl.BlockSpec(memory_space=pl.ANY)],
        out_specs=[vmem, vmem, vmem],
        scratch_shapes=[
            pltpu.VMEM((2 * spans, count, width), bf16),
            pltpu.VMEM((2 * spans, STATS, width), bf16),
            pltpu.SemaphoreType.DMA((2 * spans, 2)),
        ],
        compiler_params=pltpu.CompilerParams(vmem_limit_bytes=8 << 20),
        cost_estimate=pl.CostEstimate(
            flops=8 * spans * count * width,
            bytes_accessed=6 * spans * count * width,
            transcendentals=0,
        ),
        name="combine",
    )(owners, ranks, live, back)


def shards(hidden, norm_gain, w_query, w_out, nb_keys, nb_values, neighbours, valid_spans):
    tok_rows, width = hidden.shape
    span_dev = tok_rows // SPAN
    stored = nb_keys.shape[0]
    inner_width = w_query.shape[1]
    peer_count = lax.axis_size("dp")
    count = SPAN // PARTS
    live_span = jnp.arange(span_dev, dtype=jnp.int32) < valid_spans[0]
    owners = (neighbours // stored).reshape(-1)
    slot_ids = (neighbours % stored).reshape(-1)
    is_live = jnp.repeat(live_span, 2)
    req_order = jnp.arange(owners.shape[0], dtype=jnp.int32)
    earlier = (
        (owners[:, None] == owners[None, :])
        & is_live[None, :]
        & (req_order[None, :] < req_order[:, None])
    )
    slot_rank = jnp.minimum(jnp.sum(earlier.astype(jnp.int32), axis=1), SLOTS - 1)
    target = jnp.where(is_live, owners * SLOTS + slot_rank, -1)
    slot_match = target[:, None] == jnp.arange(peer_count * SLOTS, dtype=jnp.int32)[None, :]
    request_table = jnp.sum(jnp.where(slot_match, slot_ids[:, None], 0), axis=0)
    request_table = request_table.reshape(peer_count, SLOTS)
    source_span = jnp.sum(jnp.where(slot_match, req_order[:, None] // 2, 0), axis=0)
    wanted = lax.all_to_all(request_table, "dp", split_axis=0, concat_axis=0, tiled=True)
    wanted = wanted.reshape(-1)

    def is_last(i):
        position = i * count + lax.broadcasted_iota(jnp.int32, (1, count, 1), 1)
        return position == SPAN - 1

    def ask(i):
        queries = project(hidden, norm_gain, w_query)
        blocks = queries.reshape(span_dev, count, inner_width)
        following = shifted(blocks[:1], "dp", -1)
        grouped = jnp.concatenate([blocks[1:], following], axis=0)
        if (i + 1) * count == SPAN:
            grouped = jnp.where(is_last(i), blocks, grouped)
        sent_rows = grouped[source_span].reshape(peer_count, SLOTS * count, inner_width)
        return lax.all_to_all(sent_rows, "dp", split_axis=0, concat_axis=0, tiled=True)

    def answer(asked):
        answers = attend(wanted, asked, nb_keys, nb_values)
        return lax.all_to_all(answers, "dp", split_axis=0, concat_axis=0, tiled=True)

    def finish(i, back):
        low, high, tail = combine(owners, slot_rank, valid_spans, back)
        previous = shifted(tail, "dp", 1)
        low = low.reshape(-1, inner_width)
        row = lax.broadcasted_iota(jnp.int32, (low.shape[0], 1), 0)
        previous = jnp.pad(previous, ((0, low.shape[0] - SPAN), (0, 0)))
        low = jnp.where(row < SPAN - 1, previous, low)
        return output([low, high.reshape(-1, inner_width)], w_out).reshape(span_dev, count, width)

    asked = [ask(i) for i in range(PARTS)]
    back = [answer(one) for one in asked]
    summed = [finish(i, one) for i, one in enumerate(back)]
    summed = jnp.concatenate(summed, axis=1).reshape(tok_rows, width)
    return hidden.astype(f32) + summed


def solution(mesh):
    placed = (
        P("dp", "mp"),
        P(),
        P(None, "mp"),
        P("mp", None),
        P("dp", None, "mp"),
        P("dp", None, "mp"),
        P("dp", None),
        P("dp"),
    )
    return jax.shard_map(
        shards, mesh=mesh, in_specs=placed, out_specs=P("dp", "mp"), check_vma=False
    )
```

```python
import math

import jax
import jax.numpy as jnp
from jax import lax
from jax.experimental import pallas as pl
from jax.experimental.pallas import tpu as pltpu
from jax.sharding import PartitionSpec as P

HS = 128
SPAN = 64
SLOTS = 2
STATS = 8
PARTS = 1
LANES = 128

eps = 1e-05
f32 = jnp.float32
bf16 = jnp.bfloat16


def shifted(block, axis, distance):
    devices = range(lax.axis_size(axis))
    route = [(i - distance, i) for i in devices if i - distance in devices]
    return lax.ppermute(block, axis, route)


def turned(block, distance):
    size = lax.axis_size("mp")
    return lax.ppermute(block, "mp", [(i, (i + distance) % size) for i in range(size)])


def project(hidden, norm_gain, w_query, table):
    size = lax.axis_size("mp")
    me = lax.axis_index("mp")
    rows, width = hidden.shape
    half = rows // 2
    far = size // 2

    def weights(offset):
        start = (me + offset) % size * width
        gain = lax.dynamic_slice(norm_gain, (start,), (width,))
        part = lax.dynamic_slice(w_query, (start, 0), (width, w_query.shape[1]))
        return (part.astype(f32) * gain[:, None]).astype(bf16)

    def add(sums, h, block, weight):
        wide = block.astype(f32)
        squares = jnp.sum(wide * wide, axis=1, keepdims=True)
        product = jnp.dot(block, weight, preferred_element_type=f32)
        if sums[h] is None:
            sums[h] = (squares, product)
        else:
            sums[h] = (sums[h][0] + squares, sums[h][1] + product)

    sums = [None, None]
    halves = [hidden[:half], hidden[half:]]
    up, down = list(halves), list(halves)
    waiting = [(h, halves[h], 0) for h in range(2)]
    for step in range(1, far):
        for h in range(2):
            up[h] = turned(up[h], 1)
            down[1 - h] = turned(down[1 - h], -1)
        if step == 1:
            up[1], table = lax.optimization_barrier((up[1], table))
        else:
            for h, block, offset in waiting:
                block, up[h] = lax.optimization_barrier((block, up[h]))
                add(sums, h, block, weights(offset))
            waiting = []
        for h in range(2):
            waiting += [(h, up[h], -step), (1 - h, down[1 - h], step)]
    for h, block, offset in waiting:
        add(sums, h, block, weights(offset))
    opposite = weights(far)
    add(sums, 0, turned(up[0], 1), opposite)
    add(sums, 1, turned(down[1], -1), opposite)
    total = size * width
    return jnp.concatenate(
        [product * lax.rsqrt(squares / total + eps) for squares, product in sums], axis=0
    ).astype(bf16), table


def output(halves, w_out):
    size = lax.axis_size("mp")
    me = lax.axis_index("mp")
    width = w_out.shape[1] // size
    far = size // 2

    def term(h, offset):
        start = (me + offset) % size * width
        part = lax.dynamic_slice(w_out, (0, start), (w_out.shape[0], width))
        return jnp.dot(halves[h], part, preferred_element_type=f32)

    arrived = {}
    for step in range(far):
        new = {}
        for h, way, offset in ((1, -1, far), (1, 1, far - 1), (0, 1, far), (0, -1, far - 1)):
            offset -= step
            new[h, way] = offset > 0
            if offset > 0:
                sums = term(h, way * offset)
                if (h, way) in arrived:
                    sums = sums + arrived[h, way].astype(f32)
                arrived[h, way] = sums.astype(bf16)
        if step == 0:
            for h in range(2):
                arrived[h, 1], arrived[h, -1], halves[h] = lax.optimization_barrier(
                    (arrived[h, 1], arrived[h, -1], halves[h])
                )
        arrived = {(h, way): turned(sums, way) if new[h, way] else sums for (h, way), sums in arrived.items()}
    return jnp.concatenate(
        [term(h, 0) + arrived[h, 1].astype(f32) + arrived[h, -1].astype(f32) for h in range(2)], axis=0
    )


def attend_kernel(ids_ref, q_ref, k_ref, v_ref, out_ref):
    peers, rows, width = q_ref.shape
    count = rows // SLOTS
    together = LANES // count
    groups = width // HS // together
    step = pl.program_id(0)
    factor = 1.0 / math.sqrt(HS)
    zero = jnp.zeros((count, HS), bf16)
    row = lax.broadcasted_iota(jnp.int32, (STATS, LANES), 0)
    for p in range(peers):
        for j in range(SLOTS):
            block = ids_ref[(step * peers + p) * SLOTS + j]
            tokens = pl.ds(j * count, count)
            for g in range(groups):
                first = g * together
                cols = pl.ds(first * HS, together * HS)
                spread = []
                for h in range(together):
                    line = [zero] * together
                    line[h] = q_ref[p, tokens, pl.ds((first + h) * HS, HS)]
                    spread.append(jnp.concatenate(line, axis=1))
                scores = lax.dot_general(
                    k_ref[block, :, cols], jnp.concatenate(spread, axis=0),
                    (((1,), (1,)), ((), ())), preferred_element_type=f32,
                ) * factor
                top = jnp.max(scores, axis=0, keepdims=True)
                weights = jnp.exp(scores - top)
                total = jnp.sum(weights, axis=0, keepdims=True)
                summed = lax.dot_general(
                    weights.astype(bf16), v_ref[block, :, cols],
                    (((0,), (0,)), ((), ())), preferred_element_type=f32,
                )
                scale = jnp.transpose(jnp.broadcast_to(1.0 / total, (LANES, LANES)))
                for h in range(together):
                    own = slice(h * count, (h + 1) * count)
                    piece = summed[own, h * HS:(h + 1) * HS] * scale[own]
                    out_ref[p, tokens, pl.ds((first + h) * HS, HS)] = piece.astype(bf16)
                lse = top + jnp.log(total)
                high = lse.astype(bf16).astype(f32)
                middle = (lse - high).astype(bf16).astype(f32)
                low = (lse - high - middle).astype(bf16).astype(f32)
                stat = jnp.where(
                    row == 0, high, jnp.where(row == 1, middle, jnp.where(row == 2, low, 0.0))
                )
                place = pl.ds((g * SLOTS + j) * LANES, LANES)
                out_ref[p, pl.ds(rows, STATS), place] = stat.astype(bf16)
        used = groups * SLOTS * LANES
        if used < width:
            rest = jnp.zeros((STATS, width - used), bf16)
            out_ref[p, pl.ds(rows, STATS), pl.ds(used, width - used)] = rest


def attend(ids, asked, keys, values):
    peer_count, rows, width = asked.shape
    step = 8
    stored, tokens, _ = keys.shape
    slots = peer_count * SLOTS
    return pl.pallas_call(
        attend_kernel,
        out_shape=jax.ShapeDtypeStruct((peer_count, rows + STATS, width), bf16),
        grid_spec=pltpu.PrefetchScalarGridSpec(
            num_scalar_prefetch=1,
            grid=(peer_count // step,),
            in_specs=[
                pl.BlockSpec((step, rows, width), lambda i, ids: (i, 0, 0)),
                pl.BlockSpec((stored, tokens, width), lambda i, ids: (0, 0, 0)),
                pl.BlockSpec((stored, tokens, width), lambda i, ids: (0, 0, 0)),
            ],
            out_specs=pl.BlockSpec((step, rows + STATS, width), lambda i, ids: (i, 0, 0)),
        ),
        compiler_params=pltpu.CompilerParams(dimension_semantics=("arbitrary",)),
        cost_estimate=pl.CostEstimate(
            flops=slots * 4 * LANES * LANES * width,
            bytes_accessed=4 * peer_count * rows * width,
            transcendentals=slots * LANES * LANES,
        ),
        name="attend",
    )(ids, asked, keys, values)


def combine_kernel(
    owner_ref, rank_ref, live_ref, back_ref, low_ref, high_ref, tail_ref, part_ref, stat_ref, sems
):
    spans, count, width = part_ref.shape
    spans //= 2
    together = LANES // count
    groups = width // HS // together
    rows = SLOTS * count
    copies = []
    for i in range(2 * spans):
        offset = pl.multiple_of(rank_ref[i] * count, count)
        source = back_ref.at[owner_ref[i]]
        copies.append((
            pltpu.make_async_copy(source.at[pl.ds(offset, count)], part_ref.at[i], sems.at[i, 0]),
            pltpu.make_async_copy(source.at[pl.ds(rows, STATS)], stat_ref.at[i], sems.at[i, 1]),
        ))
    for pair in copies:
        for copy in pair:
            copy.start()
    is_last = lax.broadcasted_iota(jnp.int32, (count, HS), 0) == count - 1
    before = [jnp.zeros((count, HS), f32)] * (width // HS)
    for s in range(spans):
        for n in range(2):
            for copy in copies[2 * s + n]:
                copy.wait()
        alive = s < live_ref[0]
        block_ref = low_ref.at[s] if s < spans // 2 else high_ref.at[s - spans // 2]
        for g in range(groups):
            lses = []
            for n in range(2):
                start = pl.multiple_of((g * SLOTS + rank_ref[2 * s + n]) * LANES, LANES)
                stat = stat_ref[2 * s + n, :, pl.ds(start, LANES)].astype(f32)
                lses.append(stat[0:1] + stat[1:2] + stat[2:3])
            gap = lses[0] - lses[1]
            mine = jnp.transpose(jnp.broadcast_to(1.0 / (1.0 + jnp.exp(-gap)), (LANES, LANES)))
            other = jnp.transpose(jnp.broadcast_to(1.0 / (1.0 + jnp.exp(gap)), (LANES, LANES)))
            for h in range(together):
                own = slice(h * count, (h + 1) * count)
                head = g * together + h
                cols = pl.ds(head * HS, HS)
                merged = (
                    part_ref[2 * s, :, cols].astype(f32) * mine[own]
                    + part_ref[2 * s + 1, :, cols].astype(f32) * other[own]
                )
                merged = jnp.where(alive, merged, 0.0)
                block_ref[:, cols] = jnp.where(is_last, merged, before[head]).astype(bf16)
                before[head] = merged
                if s == spans - 1:
                    tail_ref[:, cols] = merged.astype(bf16)


def combine(owners, ranks, live, back):
    spans = owners.shape[0] // 2
    _, rows, width = back.shape
    count = (rows - STATS) // SLOTS
    smem = pl.BlockSpec(memory_space=pltpu.SMEM)
    vmem = pl.BlockSpec(memory_space=pltpu.VMEM)
    half = jax.ShapeDtypeStruct((spans // 2, count, width), bf16)
    return pl.pallas_call(
        combine_kernel,
        out_shape=[half, half, jax.ShapeDtypeStruct((count, width), bf16)],
        in_specs=[smem, smem, smem, pl.BlockSpec(memory_space=pl.ANY)],
        out_specs=[vmem, vmem, vmem],
        scratch_shapes=[
            pltpu.VMEM((2 * spans, count, width), bf16),
            pltpu.VMEM((2 * spans, STATS, width), bf16),
            pltpu.SemaphoreType.DMA((2 * spans, 2)),
        ],
        compiler_params=pltpu.CompilerParams(vmem_limit_bytes=8 << 20),
        cost_estimate=pl.CostEstimate(
            flops=8 * spans * count * width,
            bytes_accessed=6 * spans * count * width,
            transcendentals=0,
        ),
        name="combine",
    )(owners, ranks, live, back)


def shards(hidden, norm_gain, w_query, w_out, nb_keys, nb_values, neighbours, valid_spans):
    tok_rows, width = hidden.shape
    span_dev = tok_rows // SPAN
    stored = nb_keys.shape[0]
    inner_width = w_query.shape[1]
    peer_count = lax.axis_size("dp")
    count = SPAN // PARTS
    live_span = jnp.arange(span_dev, dtype=jnp.int32) < valid_spans[0]
    owners = (neighbours // stored).reshape(-1)
    slot_ids = (neighbours % stored).reshape(-1)
    is_live = jnp.repeat(live_span, 2)
    req_order = jnp.arange(owners.shape[0], dtype=jnp.int32)
    earlier = (
        (owners[:, None] == owners[None, :])
        & is_live[None, :]
        & (req_order[None, :] < req_order[:, None])
    )
    slot_rank = jnp.minimum(jnp.sum(earlier.astype(jnp.int32), axis=1), SLOTS - 1)
    target = jnp.where(is_live, owners * SLOTS + slot_rank, -1)
    slot_match = target[:, None] == jnp.arange(peer_count * SLOTS, dtype=jnp.int32)[None, :]
    request_table = jnp.sum(jnp.where(slot_match, slot_ids[:, None], 0), axis=0)
    request_table = request_table.reshape(peer_count, SLOTS)
    source_span = jnp.sum(jnp.where(slot_match, req_order[:, None] // 2, 0), axis=0)
    def is_last(i):
        position = i * count + lax.broadcasted_iota(jnp.int32, (1, count, 1), 1)
        return position == SPAN - 1

    def ask(i):
        queries, table = project(hidden, norm_gain, w_query, request_table)
        blocks = queries.reshape(span_dev, count, inner_width)
        following = shifted(blocks[:1], "dp", -1)
        grouped = jnp.concatenate([blocks[1:], following], axis=0)
        if (i + 1) * count == SPAN:
            grouped = jnp.where(is_last(i), blocks, grouped)
        sent_rows = grouped[source_span].reshape(peer_count, SLOTS * count, inner_width)
        wanted = lax.all_to_all(table, "dp", split_axis=0, concat_axis=0, tiled=True).reshape(-1)
        return wanted, lax.all_to_all(sent_rows, "dp", split_axis=0, concat_axis=0, tiled=True)

    def answer(request):
        wanted, asked = request
        answers = attend(wanted, asked, nb_keys, nb_values)
        return lax.all_to_all(answers, "dp", split_axis=0, concat_axis=0, tiled=True)

    def finish(i, back):
        low, high, tail = combine(owners, slot_rank, valid_spans, back)
        previous = shifted(tail, "dp", 1)
        low = low.reshape(-1, inner_width)
        row = lax.broadcasted_iota(jnp.int32, (low.shape[0], 1), 0)
        previous = jnp.pad(previous, ((0, low.shape[0] - SPAN), (0, 0)))
        low = jnp.where(row < SPAN - 1, previous, low)
        return output([low, high.reshape(-1, inner_width)], w_out).reshape(span_dev, count, width)

    asked = [ask(i) for i in range(PARTS)]
    back = [answer(one) for one in asked]
    summed = [finish(i, one) for i, one in enumerate(back)]
    summed = jnp.concatenate(summed, axis=1).reshape(tok_rows, width)
    return hidden.astype(f32) + summed


def solution(mesh):
    placed = (
        P("dp", "mp"),
        P(),
        P(None, "mp"),
        P("mp", None),
        P("dp", None, "mp"),
        P("dp", None, "mp"),
        P("dp", None),
        P("dp"),
    )
    return jax.shard_map(
        shards, mesh=mesh, in_specs=placed, out_specs=P("dp", "mp"), check_vma=False
    )
```

```python
import math

import jax
import jax.numpy as jnp
from jax import lax
from jax.experimental import pallas as pl
from jax.experimental.pallas import tpu as pltpu
from jax.sharding import PartitionSpec as P

HS = 128
SPAN = 64
SLOTS = 2
STATS = 8
PARTS = 1
LANES = 128

eps = 1e-05
f32 = jnp.float32
bf16 = jnp.bfloat16


def shifted(block, axis, distance):
    devices = range(lax.axis_size(axis))
    route = [(i - distance, i) for i in devices if i - distance in devices]
    return lax.ppermute(block, axis, route)


def turned(block, distance):
    size = lax.axis_size("mp")
    return lax.ppermute(block, "mp", [(i, (i + distance) % size) for i in range(size)])


def project(hidden, norm_gain, w_query, table):
    size = lax.axis_size("mp")
    me = lax.axis_index("mp")
    rows, width = hidden.shape
    half = rows // 2
    far = size // 2

    def weights(offset):
        start = (me + offset) % size * width
        gain = lax.dynamic_slice(norm_gain, (start,), (width,))
        part = lax.dynamic_slice(w_query, (start, 0), (width, w_query.shape[1]))
        return (part.astype(f32) * gain[:, None]).astype(bf16)

    def add(sums, h, block, weight):
        wide = block.astype(f32)
        squares = jnp.sum(wide * wide, axis=1, keepdims=True)
        product = jnp.dot(block, weight, preferred_element_type=f32)
        if sums[h] is None:
            sums[h] = (squares, product)
        else:
            sums[h] = (sums[h][0] + squares, sums[h][1] + product)

    sums = [None, None]
    halves = [hidden[:half], hidden[half:]]
    up, down = list(halves), list(halves)
    waiting = [(h, halves[h], 0) for h in range(2)]
    for step in range(1, far):
        for h in range(2):
            up[h] = turned(up[h], 1)
            down[1 - h] = turned(down[1 - h], -1)
        if step > 1:
            for h, block, offset in waiting:
                block, up[h] = lax.optimization_barrier((block, up[h]))
                add(sums, h, block, weights(offset))
            waiting = []
        for h in range(2):
            waiting += [(h, up[h], -step), (1 - h, down[1 - h], step)]
    for h, block, offset in waiting:
        add(sums, h, block, weights(offset))
    opposite = weights(far)
    add(sums, 0, turned(up[0], 1), opposite)
    add(sums, 1, turned(down[1], -1), opposite)
    total = size * width
    return jnp.concatenate(
        [product * lax.rsqrt(squares / total + eps) for squares, product in sums], axis=0
    ).astype(bf16), table


def output(halves, w_out):
    size = lax.axis_size("mp")
    me = lax.axis_index("mp")
    width = w_out.shape[1] // size
    far = size // 2

    def term(h, offset):
        start = (me + offset) % size * width
        part = lax.dynamic_slice(w_out, (0, start), (w_out.shape[0], width))
        return jnp.dot(halves[h], part, preferred_element_type=f32)

    arrived = {}
    for step in range(far):
        new = {}
        for h, way, offset in ((1, -1, far), (1, 1, far - 1), (0, 1, far), (0, -1, far - 1)):
            offset -= step
            new[h, way] = offset > 0
            if offset > 0:
                sums = term(h, way * offset)
                if (h, way) in arrived:
                    sums = sums + arrived[h, way].astype(f32)
                arrived[h, way] = sums.astype(bf16)
        if step == 0:
            for h in range(2):
                arrived[h, 1], arrived[h, -1], halves[h] = lax.optimization_barrier(
                    (arrived[h, 1], arrived[h, -1], halves[h])
                )
        arrived = {(h, way): turned(sums, way) if new[h, way] else sums for (h, way), sums in arrived.items()}
    return jnp.concatenate(
        [term(h, 0) + arrived[h, 1].astype(f32) + arrived[h, -1].astype(f32) for h in range(2)], axis=0
    )


def attend_kernel(ids_ref, q_ref, k_ref, v_ref, out_ref):
    peers, rows, width = q_ref.shape
    count = rows // SLOTS
    together = LANES // count
    groups = width // HS // together
    step = pl.program_id(0)
    factor = 1.0 / math.sqrt(HS)
    zero = jnp.zeros((count, HS), bf16)
    row = lax.broadcasted_iota(jnp.int32, (STATS, LANES), 0)
    for p in range(peers):
        for j in range(SLOTS):
            block = ids_ref[(step * peers + p) * SLOTS + j]
            tokens = pl.ds(j * count, count)
            for g in range(groups):
                first = g * together
                cols = pl.ds(first * HS, together * HS)
                spread = []
                for h in range(together):
                    line = [zero] * together
                    line[h] = q_ref[p, tokens, pl.ds((first + h) * HS, HS)]
                    spread.append(jnp.concatenate(line, axis=1))
                scores = lax.dot_general(
                    k_ref[block, :, cols], jnp.concatenate(spread, axis=0),
                    (((1,), (1,)), ((), ())), preferred_element_type=f32,
                ) * factor
                top = jnp.max(scores, axis=0, keepdims=True)
                weights = jnp.exp(scores - top)
                total = jnp.sum(weights, axis=0, keepdims=True)
                summed = lax.dot_general(
                    weights.astype(bf16), v_ref[block, :, cols],
                    (((0,), (0,)), ((), ())), preferred_element_type=f32,
                )
                scale = jnp.transpose(jnp.broadcast_to(1.0 / total, (LANES, LANES)))
                for h in range(together):
                    own = slice(h * count, (h + 1) * count)
                    piece = summed[own, h * HS:(h + 1) * HS] * scale[own]
                    out_ref[p, tokens, pl.ds((first + h) * HS, HS)] = piece.astype(bf16)
                lse = top + jnp.log(total)
                high = lse.astype(bf16).astype(f32)
                middle = (lse - high).astype(bf16).astype(f32)
                low = (lse - high - middle).astype(bf16).astype(f32)
                stat = jnp.where(
                    row == 0, high, jnp.where(row == 1, middle, jnp.where(row == 2, low, 0.0))
                )
                place = pl.ds((g * SLOTS + j) * LANES, LANES)
                out_ref[p, pl.ds(rows, STATS), place] = stat.astype(bf16)
        used = groups * SLOTS * LANES
        if used < width:
            rest = jnp.zeros((STATS, width - used), bf16)
            out_ref[p, pl.ds(rows, STATS), pl.ds(used, width - used)] = rest


def attend(ids, asked, keys, values):
    peer_count, rows, width = asked.shape
    step = 8
    stored, tokens, _ = keys.shape
    slots = peer_count * SLOTS
    return pl.pallas_call(
        attend_kernel,
        out_shape=jax.ShapeDtypeStruct((peer_count, rows + STATS, width), bf16),
        grid_spec=pltpu.PrefetchScalarGridSpec(
            num_scalar_prefetch=1,
            grid=(peer_count // step,),
            in_specs=[
                pl.BlockSpec((step, rows, width), lambda i, ids: (i, 0, 0)),
                pl.BlockSpec((stored, tokens, width), lambda i, ids: (0, 0, 0)),
                pl.BlockSpec((stored, tokens, width), lambda i, ids: (0, 0, 0)),
            ],
            out_specs=pl.BlockSpec((step, rows + STATS, width), lambda i, ids: (i, 0, 0)),
        ),
        compiler_params=pltpu.CompilerParams(dimension_semantics=("arbitrary",)),
        cost_estimate=pl.CostEstimate(
            flops=slots * 4 * LANES * LANES * width,
            bytes_accessed=4 * peer_count * rows * width,
            transcendentals=slots * LANES * LANES,
        ),
        name="attend",
    )(ids, asked, keys, values)


def combine_kernel(
    owner_ref, rank_ref, live_ref, back_ref, low_ref, high_ref, tail_ref, part_ref, stat_ref, sems
):
    spans, count, width = part_ref.shape
    spans //= 2
    together = LANES // count
    groups = width // HS // together
    rows = SLOTS * count
    copies = []
    for i in range(2 * spans):
        offset = pl.multiple_of(rank_ref[i] * count, count)
        source = back_ref.at[owner_ref[i]]
        copies.append((
            pltpu.make_async_copy(source.at[pl.ds(offset, count)], part_ref.at[i], sems.at[i, 0]),
            pltpu.make_async_copy(source.at[pl.ds(rows, STATS)], stat_ref.at[i], sems.at[i, 1]),
        ))
    for pair in copies:
        for copy in pair:
            copy.start()
    is_last = lax.broadcasted_iota(jnp.int32, (count, HS), 0) == count - 1
    before = [jnp.zeros((count, HS), f32)] * (width // HS)
    for s in range(spans):
        for n in range(2):
            for copy in copies[2 * s + n]:
                copy.wait()
        alive = s < live_ref[0]
        block_ref = low_ref.at[s] if s < spans // 2 else high_ref.at[s - spans // 2]
        for g in range(groups):
            lses = []
            for n in range(2):
                start = pl.multiple_of((g * SLOTS + rank_ref[2 * s + n]) * LANES, LANES)
                stat = stat_ref[2 * s + n, :, pl.ds(start, LANES)].astype(f32)
                lses.append(stat[0:1] + stat[1:2] + stat[2:3])
            gap = lses[0] - lses[1]
            mine = jnp.transpose(jnp.broadcast_to(1.0 / (1.0 + jnp.exp(-gap)), (LANES, LANES)))
            other = jnp.transpose(jnp.broadcast_to(1.0 / (1.0 + jnp.exp(gap)), (LANES, LANES)))
            for h in range(together):
                own = slice(h * count, (h + 1) * count)
                head = g * together + h
                cols = pl.ds(head * HS, HS)
                merged = (
                    part_ref[2 * s, :, cols].astype(f32) * mine[own]
                    + part_ref[2 * s + 1, :, cols].astype(f32) * other[own]
                )
                merged = jnp.where(alive, merged, 0.0)
                block_ref[:, cols] = jnp.where(is_last, merged, before[head]).astype(bf16)
                before[head] = merged
                if s == spans - 1:
                    tail_ref[:, cols] = merged.astype(bf16)


def combine(owners, ranks, live, back):
    spans = owners.shape[0] // 2
    _, rows, width = back.shape
    count = (rows - STATS) // SLOTS
    smem = pl.BlockSpec(memory_space=pltpu.SMEM)
    vmem = pl.BlockSpec(memory_space=pltpu.VMEM)
    half = jax.ShapeDtypeStruct((spans // 2, count, width), bf16)
    return pl.pallas_call(
        combine_kernel,
        out_shape=[half, half, jax.ShapeDtypeStruct((count, width), bf16)],
        in_specs=[smem, smem, smem, pl.BlockSpec(memory_space=pl.ANY)],
        out_specs=[vmem, vmem, vmem],
        scratch_shapes=[
            pltpu.VMEM((2 * spans, count, width), bf16),
            pltpu.VMEM((2 * spans, STATS, width), bf16),
            pltpu.SemaphoreType.DMA((2 * spans, 2)),
        ],
        compiler_params=pltpu.CompilerParams(vmem_limit_bytes=8 << 20),
        cost_estimate=pl.CostEstimate(
            flops=8 * spans * count * width,
            bytes_accessed=6 * spans * count * width,
            transcendentals=0,
        ),
        name="combine",
    )(owners, ranks, live, back)


def shards(hidden, norm_gain, w_query, w_out, nb_keys, nb_values, neighbours, valid_spans):
    tok_rows, width = hidden.shape
    span_dev = tok_rows // SPAN
    stored = nb_keys.shape[0]
    inner_width = w_query.shape[1]
    peer_count = lax.axis_size("dp")
    count = SPAN // PARTS
    live_span = jnp.arange(span_dev, dtype=jnp.int32) < valid_spans[0]
    owners = (neighbours // stored).reshape(-1)
    slot_ids = (neighbours % stored).reshape(-1)
    is_live = jnp.repeat(live_span, 2)
    req_order = jnp.arange(owners.shape[0], dtype=jnp.int32)
    earlier = (
        (owners[:, None] == owners[None, :])
        & is_live[None, :]
        & (req_order[None, :] < req_order[:, None])
    )
    slot_rank = jnp.minimum(jnp.sum(earlier.astype(jnp.int32), axis=1), SLOTS - 1)
    target = jnp.where(is_live, owners * SLOTS + slot_rank, -1)
    slot_match = target[:, None] == jnp.arange(peer_count * SLOTS, dtype=jnp.int32)[None, :]
    request_table = jnp.sum(jnp.where(slot_match, slot_ids[:, None], 0), axis=0)
    request_table = request_table.reshape(peer_count, SLOTS)
    source_span = jnp.sum(jnp.where(slot_match, req_order[:, None] // 2, 0), axis=0)
    def is_last(i):
        position = i * count + lax.broadcasted_iota(jnp.int32, (1, count, 1), 1)
        return position == SPAN - 1

    def ask(i):
        queries, table = project(hidden, norm_gain, w_query, request_table)
        blocks = queries.reshape(span_dev, count, inner_width)
        following = shifted(blocks[:1], "dp", -1)
        grouped = jnp.concatenate([blocks[1:], following], axis=0)
        if (i + 1) * count == SPAN:
            grouped = jnp.where(is_last(i), blocks, grouped)
        sent_rows = grouped[source_span].reshape(peer_count, SLOTS * count, inner_width)
        wanted = lax.all_to_all(table, "dp", split_axis=0, concat_axis=0, tiled=True).reshape(-1)
        return wanted, lax.all_to_all(sent_rows, "dp", split_axis=0, concat_axis=0, tiled=True)

    def answer(request):
        wanted, asked = request
        answers = attend(wanted, asked, nb_keys, nb_values)
        return lax.all_to_all(answers, "dp", split_axis=0, concat_axis=0, tiled=True)

    def finish(i, back):
        low, high, tail = combine(owners, slot_rank, valid_spans, back)
        previous = shifted(tail, "dp", 1)
        low = low.reshape(-1, inner_width)
        row = lax.broadcasted_iota(jnp.int32, (low.shape[0], 1), 0)
        previous = jnp.pad(previous, ((0, low.shape[0] - SPAN), (0, 0)))
        low = jnp.where(row < SPAN - 1, previous, low)
        return output([low, high.reshape(-1, inner_width)], w_out).reshape(span_dev, count, width)

    asked = [ask(i) for i in range(PARTS)]
    back = [answer(one) for one in asked]
    summed = [finish(i, one) for i, one in enumerate(back)]
    summed = jnp.concatenate(summed, axis=1).reshape(tok_rows, width)
    return hidden.astype(f32) + summed


def solution(mesh):
    placed = (
        P("dp", "mp"),
        P(),
        P(None, "mp"),
        P("mp", None),
        P("dp", None, "mp"),
        P("dp", None, "mp"),
        P("dp", None),
        P("dp"),
    )
    return jax.shard_map(
        shards, mesh=mesh, in_specs=placed, out_specs=P("dp", "mp"), check_vma=False
    )
```
